256 devices in a mesh: group: 32 (over x, z), span: 8 (over y, core).
Axes of the slice: x: 4, y: 4, z: 8, core: 2. Of those that a mesh axis runs over, the one named last changes fastest.
Arguments:
- struct_disp: float32 [3, 524288], P(None, ('group', 'span')), may hold values from -6 to 6
- interp_weight: float32 [524288, 4], P(('group', 'span')), may hold values from 0.2 to 1
- face_owner: int32 [524288, 4], P(('group', 'span')), may hold values from 0 to 31, all different within a row; in each aligned block of 2048 rows (0 to 2047, 2048 to 4095, ...) at most 512 rows name the same one
- face_row: int32 [524288, 4], P(('group', 'span')), may hold values from 0 to 20479
- skel_force: float32 [3, 16384], P(None, ('group', 'span')), may hold values from -6 to 6
- skel_coupling: float32 [6, 16384], P(None, ('group', 'span')), may hold values from 0.1 to 0.2
- skel_stiff: float32 [16384], P(('group', 'span')), may hold values from 0.05 to 0.15
- skel_edges: int32 [6, 16384], P(None, ('group', 'span')), may hold values from 0 to 16383
- block_spacing: float32 [3, 256], P(None, 'group'), may hold values from 1 to 2
Outputs:
- displacement: float32 [3, 256, 64, 6400], P(None, 'group', 'span')
- jacobian: float32 [256, 64, 6400], P('group', 'span')
The draws below stay inside these ranges and needn't reach their ends.
Inputs may be any that keep to these rules, and one draw needn't show every extreme that they name: `face_owner`: each row names 4 different group indices; among the rows of one device no index is named more than 512 times, a bound that some block reaches.
All inputs are finite; a program needn't handle non-finite values.
Results may differ from the reference program's by a relative error of at most 0.0001.
Values sent between devices are 32-bit elements; how exact they have to be, the bound alone decides.
A program may use at most 128 MiB of HBM per device.

```python
import math
import jax
import jax.numpy as jnp
import numpy as np
from jax import lax

SN_DEV = 2048
TOPW = 4
BPD = 8
SPAN_DEV = 8
NP = 80
DEG = 6
ITERS = 4
EDGE = 320
FROWS = 20480
CAP = 512
NS = 524288
NK = 16384
BLOCKS = 256
SPANS = 64
N_GROUP = 32
N_SPAN = 8


def with_ends(array, own_key, smallest, top_value):
    longest = array.shape.index(max(array.shape))
    spots = []
    for shift in (0, 1):
        where = [jax.random.randint(jax.random.fold_in(own_key, axis), (), 0, length) for axis, length in enumerate(array.shape)]
        where[longest] = (where[longest] + shift) % array.shape[longest]
        spots.append(tuple(where))
    return array.at[spots[0]].set(smallest).at[spots[1]].set(top_value)


def block_scale(key, extent, pieces, low, high):
    def one(dim, blocks):
        heights = jax.random.uniform(jax.random.fold_in(jax.random.fold_in(key, 6), dim), (blocks,), jnp.float32, low / len(pieces), high / len(pieces))
        return jnp.repeat(jnp.exp(heights), extent[dim] // blocks).reshape((-1,) + (1,) * (len(extent) - dim - 1))

    loudness = one(*pieces[0])
    for cut in pieces[1:]:
        loudness = loudness * one(*cut)
    return loudness


def routed_block(stream_key, own, number, rows, count, top, bound, skew):
    sequence = jax.random.permutation(stream_key, count)
    heavy_load, usual = shares(count, rows * top, bound, skew, True), shares(count, rows * top, bound, skew, False)
    places = jnp.arange(count)

    def named(tallies, turn):
        used = int((tallies > 0).sum())
        fixed = max(1, used // 4)
        shifted = fixed + (places - fixed + turn * (used - fixed)) % max(1, count - fixed)
        return jnp.zeros((count,), jnp.int32).at[sequence[jnp.where(places < fixed, places, shifted)]].set(jnp.asarray(tallies, jnp.int32))

    tallies = jnp.where(number % 4 == 0, named(heavy_load, number // 4), named(usual, number - number // 4 - 1))
    mixed = jax.random.permutation(jax.random.fold_in(own, 3), count)
    donor, sink = mixed[0:count // 2 * 2:2], mixed[1:count // 2 * 2:2]
    margin = jnp.minimum(tallies[donor] - 1, bound - tallies[sink]) // 2
    margin = jnp.where((donor == sequence[0]) | (sink == sequence[0]) | (tallies[sink] == 0), 0, jnp.maximum(margin, 0))
    shifted = jax.random.randint(jax.random.fold_in(own, 4), (count // 2,), 0, 1 << 20) % (margin + 1)
    tallies = tallies.at[donor].add(-shifted).at[sink].add(shifted)
    labels = jnp.searchsorted(jnp.cumsum(tallies), jnp.arange(rows * top), side="right").astype(jnp.int32)
    grid = labels.reshape(top, rows).T
    grid = grid[jax.random.permutation(jax.random.fold_in(own, 1), rows)]
    turn = jax.random.randint(jax.random.fold_in(own, 2), (rows, 1), 0, top)
    return jnp.take_along_axis(grid, (jnp.arange(top)[None, :] + turn) % top, axis=1)


def shares(count, total, limit, slope, full):
    loads = [(1 << 20) // math.isqrt(grade ** slope) + 1 for grade in range(1, count + 1)]
    largest = limit if full else min(limit, max(-(-total // count), total * loads[0] // sum(loads)))
    least = 1 if total - largest >= count - 1 else 0
    holding, rest = [largest] + [least] * (count - 1), total - largest - least * (count - 1)
    while rest > 0:
        free = [i for i in range(1, count) if holding[i] < largest] or [i for i in range(1, count) if holding[i] < limit]
        mass, left = sum([loads[i] for i in free]), rest
        for i in free:
            more = min(limit - holding[i], max(1, left * loads[i] // mass), rest)
            holding[i] = holding[i] + more
            rest = rest - more
    return np.array(holding)


def centred(own_key, dims, width, most, pieces=(), kind=jnp.bfloat16):
    result = jax.random.normal(own_key, dims, jnp.float32) * width
    if len(pieces) > 0:
        result = block_scale(own_key, dims, pieces, -0.22, 0.18) * result
    return jnp.clip(result, min=-most, max=most).astype(kind)


def setup_inputs(seed: int = 0) -> dict:
    seeds = jax.random.split(jax.random.key(seed), 10)
    struct_disp = centred(seeds[0], (3, NS), 1.0, 6.0, ((1, 256),), jnp.float32)
    interp_weight = jnp.clip(0.2 + 0.8 * jax.random.uniform(seeds[1], (NS, TOPW), jnp.float32) ** block_scale(seeds[1], (NS, TOPW), ((0, 256),), -0.2, 0.2), 0.2, 1.0)
    face_owner_keys = jax.random.split(jax.random.fold_in(seeds[2], 1), NS // SN_DEV)
    face_owner_turns = jax.random.permutation(jax.random.fold_in(seeds[2], 3), NS // SN_DEV)
    face_owner = jax.vmap(lambda own, number: routed_block(jax.random.fold_in(seeds[2], 2), own, number, SN_DEV, N_GROUP, TOPW, CAP, 2))(face_owner_keys, face_owner_turns).reshape((NS, TOPW))
    face_row = with_ends(jax.random.randint(seeds[3], (NS, TOPW), 0, FROWS), jax.random.fold_in(seeds[3], 1), 0, FROWS - 1).astype(jnp.int32)
    skel_force = centred(seeds[4], (3, NK), 1.0, 6.0, ((1, 256),), jnp.float32)
    skel_coupling = jnp.clip(0.1 + 0.1 * jax.random.uniform(seeds[5], (DEG, NK), jnp.float32) ** block_scale(seeds[5], (DEG, NK), ((1, 256),), -0.2, 0.2), 0.1, 0.2)
    skel_stiff = jnp.clip(jnp.exp(math.log(0.15) - 1.0986123 * jax.random.uniform(seeds[6], (NK,), jnp.float32) ** block_scale(seeds[6], (NK,), ((0, 256),), -0.2, 0.2)), 0.05, 0.15)
    skel_edges = with_ends(jax.random.randint(seeds[7], (DEG, NK), 0, NK), jax.random.fold_in(seeds[7], 1), 0, NK - 1).astype(jnp.int32)
    block_spacing = jnp.clip(jnp.exp(math.log(2.0) - 0.6931472 * jax.random.uniform(seeds[8], (3, BLOCKS), jnp.float32) ** block_scale(seeds[8], (3, BLOCKS), ((1, 32),), -0.2, 0.2)), 1.0, 2.0)
    return {"struct_disp": struct_disp, "interp_weight": interp_weight, "face_owner": face_owner, "face_row": face_row, "skel_force": skel_force, "skel_coupling": skel_coupling, "skel_stiff": skel_stiff, "skel_edges": skel_edges, "block_spacing": block_spacing}


def tfi_tables(points):
    position = jnp.arange(points * points, dtype=jnp.int32)
    first = position % points
    second = position // points
    frac_first = first.astype(jnp.float32) / (points - 1)
    frac_second = second.astype(jnp.float32) / (points - 1)
    edge_pos = jnp.arange(points, dtype=jnp.int32)[:, None]
    zero = jnp.zeros((points, points * points), jnp.float32)
    bottom = jnp.where(first[None] == edge_pos, (1.0 - frac_second)[None], zero)
    bottom = bottom.at[0].add(-(1.0 - frac_first) * (1.0 - frac_second))
    bottom = bottom.at[points - 1].add(-frac_first * (1.0 - frac_second))
    top_rows = jnp.where(first[None] == edge_pos, frac_second[None], zero)
    top_rows = top_rows.at[0].add(-(1.0 - frac_first) * frac_second)
    top_rows = top_rows.at[points - 1].add(-frac_first * frac_second)
    left_rows = jnp.where(second[None] == edge_pos, (1.0 - frac_first)[None], zero)
    right_rows = jnp.where(second[None] == edge_pos, frac_first[None], zero)
    table = jnp.concatenate([bottom, top_rows, left_rows, right_rows], axis=0)
    bubble = 16.0 * frac_first * (1.0 - frac_first) * frac_second * (1.0 - frac_second)
    return table, bubble


def plane_derivs(field, points):
    position = jnp.arange(points * points, dtype=jnp.int32)
    first = position % points
    second = position // points
    ahead = jnp.concatenate([field[..., 1:], field[..., -1:]], axis=-1)
    behind = jnp.concatenate([field[..., :1], field[..., :-1]], axis=-1)
    deriv_first = (jnp.where(first == points - 1, field, ahead) - jnp.where(first == 0, field, behind)) * 0.5
    upper = jnp.concatenate([field[..., points:], field[..., -points:]], axis=-1)
    lower = jnp.concatenate([field[..., :points], field[..., :-points]], axis=-1)
    deriv_second = (jnp.where(second == points - 1, field, upper) - jnp.where(second == 0, field, lower)) * 0.5
    return deriv_first, deriv_second


def metric_det(spacing, deriv_first, deriv_second, deriv_span):
    derivs = (deriv_first, deriv_second, deriv_span)
    matrix = [[derivs[col][row] for col in range(3)] for row in range(3)]
    for row in range(3):
        matrix[row][row] = matrix[row][row] + spacing[row][:, None, None]
    minor_one = matrix[1][1] * matrix[2][2] - matrix[1][2] * matrix[2][1]
    minor_two = matrix[1][0] * matrix[2][2] - matrix[1][2] * matrix[2][0]
    minor_three = matrix[1][0] * matrix[2][1] - matrix[1][1] * matrix[2][0]
    return matrix[0][0] * minor_one - matrix[0][1] * minor_two + matrix[0][2] * minor_three


def reference(struct_disp, interp_weight, face_owner, face_row, skel_force, skel_coupling, skel_stiff, skel_edges, block_spacing):
    node_ids = jnp.arange(NS, dtype=jnp.int32)
    node_span = (node_ids // SN_DEV) % N_SPAN
    owner_flat = face_owner * N_SPAN + node_span[:, None]
    target_rows = (owner_flat * FROWS + face_row).reshape(-1)
    weighted = (struct_disp[:, :, None] * interp_weight[None]).reshape(3, -1)
    face_disp = jnp.zeros((3, FROWS * N_GROUP * N_SPAN), jnp.float32).at[:, target_rows].add(weighted)
    face_disp = face_disp.reshape(3, N_GROUP, N_SPAN, BPD, SPAN_DEV, EDGE)
    face_disp = face_disp.transpose(0, 1, 3, 2, 4, 5).reshape(3, BLOCKS, SPANS, EDGE)
    face_load = 0.25 * jnp.sum(face_disp, axis=3)
    face_load = face_load.reshape(3, N_GROUP, BPD, N_SPAN, SPAN_DEV).transpose(0, 1, 3, 2, 4).reshape(3, NK)
    skeleton_rhs = skel_force + face_load
    diagonal = skel_stiff + jnp.sum(skel_coupling, axis=0)

    def sweep(sweep_index, state):
        neighbours = state[:, skel_edges]
        return (skeleton_rhs + jnp.sum(skel_coupling[None] * neighbours, axis=1)) / diagonal

    skeleton = lax.fori_loop(0, ITERS, sweep, jnp.zeros((3, NK), jnp.float32))
    skeleton = skeleton.reshape(3, N_GROUP, N_SPAN, BPD, SPAN_DEV).transpose(0, 1, 3, 2, 4).reshape(3, BLOCKS, SPANS)
    table, bubble = tfi_tables(NP)
    blended = jnp.einsum("cbke,ef->cbkf", face_disp, table, precision=lax.Precision.HIGHEST)
    displacement = blended + skeleton[..., None] * bubble
    deriv_first, deriv_second = plane_derivs(displacement, NP)
    padded = jnp.pad(displacement, ((0, 0), (0, 0), (1, 1), (0, 0)))
    deriv_span = (padded[:, :, 2:] - padded[:, :, :-2]) * 0.5
    jacobian = metric_det(block_spacing, deriv_first, deriv_second, deriv_span)
    return displacement, jacobian
```

```python
import functools

import jax
import jax.numpy as jnp
import numpy as np
from jax import lax
from jax.experimental import pallas as pl
from jax.experimental.pallas import tpu as pltpu
from jax.sharding import PartitionSpec as P

F32, BF16, I32 = jnp.float32, jnp.bfloat16, jnp.int32
NP = 80
LAYERS = 64
GROUPS, SPANS = 32, 8
NODES = 2048
MESH = pl.DeviceIdType.MESH
NT = (((1,), (1,)), ((), ()))
VMEM_SPEC = pl.BlockSpec(memory_space=pltpu.VMEM)


def iota(shape, dim):
    return lax.broadcasted_iota(I32, shape, dim)


def split(value):
    high = value.astype(BF16)
    return high, (value - high.astype(F32)).astype(BF16)


def pack_body(disp_ref, weight_ref, owner_ref, row_ref, out_ref, lhs, rhs):
    group_rows = iota((GROUPS, NODES), 0)
    present = jnp.zeros((GROUPS, NODES), F32)
    for t in range(4):
        present += jnp.where(owner_ref[t : t + 1, :] == group_rows, 1.0, 0.0)
    present = present.astype(BF16)
    before = jnp.where(iota((256, 256), 0) < iota((256, 256), 1), 1.0, 0.0).astype(BF16)
    every = jnp.ones((256, 256), BF16)
    base = jnp.zeros((GROUPS, 256), F32)
    ranks = []
    for k in range(NODES // 256):
        piece = present[:, k * 256 : (k + 1) * 256]
        ranks.append(jnp.dot(piece, before, preferred_element_type=F32) + base)
        base += jnp.dot(piece, every, preferred_element_type=F32)
    rank = jnp.concatenate(ranks, axis=1)
    word = iota((8, NODES), 0) & 3
    total = jnp.zeros((512, 256), F32)
    for t in range(4):
        owner = owner_ref[t : t + 1, :]
        slot = jnp.sum(jnp.where(owner == group_rows, rank, 0.0), axis=0, keepdims=True).astype(I32)
        half = slot >> 8
        column = slot & 255
        bucket = owner * 2 + half
        row = row_ref[t : t + 1, :]
        layer = ((row >> 6) * 205) >> 10
        edge = row - layer * (4 * NP)
        seg = ((edge >> 4) * 205) >> 10
        along = (edge - seg * NP) << 8
        line = seg * LAYERS + layer
        weight = weight_ref[t : t + 1, :]
        value = jnp.where(
            word == 0, disp_ref[0:1, :], jnp.where(word == 1, disp_ref[1:2, :], disp_ref[2:3, :])
        ) * weight
        high = jnp.where(word == 3, along.astype(F32), value).astype(BF16)
        low = jnp.where(word == 3, line.astype(F32), value - high.astype(F32)).astype(BF16)
        high = jnp.concatenate([high] * 32, axis=0)
        low = jnp.concatenate([low] * 32, axis=0)
        hit = (iota((256, NODES), 0) >> 2) == bucket
        zero = jnp.zeros((), BF16)
        lhs[0:256, :] = jnp.where(hit, high, zero)
        lhs[256:512, :] = jnp.where(hit, low, zero)
        rhs[...] = jnp.where(iota((256, NODES), 0) == column, 1.0, 0.0).astype(BF16)
        total += lax.dot_general(lhs[...], rhs[...], NT, preferred_element_type=F32)
    out_ref[...] = (total[0:256] + total[256:512]).reshape(GROUPS, 8, 256)


def pack(disp, weight, owner, row):
    return pl.pallas_call(
        pack_body,
        name="pack",
        out_shape=jax.ShapeDtypeStruct((GROUPS, 8, 256), F32),
        in_specs=[VMEM_SPEC] * 4,
        out_specs=VMEM_SPEC,
        scratch_shapes=[pltpu.VMEM((512, NODES), BF16), pltpu.VMEM((256, NODES), BF16)],
        compiler_params=pltpu.CompilerParams(vmem_limit_bytes=48 << 20),
    )(disp, weight, owner, row)


def wait_for(ref, sem):
    pltpu.make_async_copy(ref, ref, sem).wait()


def exchange_body(send_ref, recv_ref, send_sem, recv_sem, own_sem):
    g, s = lax.axis_index("group"), lax.axis_index("span")
    barrier = pltpu.get_barrier_semaphore()

    def greet(k, carry):
        pl.semaphore_signal(barrier, inc=1, device_id=((g + k) % GROUPS, s), device_id_type=MESH)
        return carry

    lax.fori_loop(1, GROUPS, greet, 0)
    pl.semaphore_wait(barrier, GROUPS - 1)
    own = pltpu.make_async_copy(send_ref.at[g], recv_ref.at[g], own_sem)
    own.start()

    def push(k, carry):
        peer = (g + k) % GROUPS
        pltpu.make_async_remote_copy(
            send_ref.at[peer],
            recv_ref.at[g],
            send_sem,
            recv_sem,
            device_id=(peer, s),
            device_id_type=MESH,
        ).start()
        return carry

    lax.fori_loop(1, GROUPS, push, 0)
    own.wait()
    wait_for(recv_ref.at[pl.ds(0, GROUPS - 1)], recv_sem)
    wait_for(send_ref.at[pl.ds(0, GROUPS - 1)], send_sem)


def exchange(send):
    return pl.pallas_call(
        exchange_body,
        name="exchange",
        out_shape=jax.ShapeDtypeStruct((GROUPS, 8, 256), F32),
        in_specs=[VMEM_SPEC],
        out_specs=VMEM_SPEC,
        scratch_shapes=[pltpu.SemaphoreType.DMA] * 3,
        compiler_params=pltpu.CompilerParams(collective_id=0, has_side_effects=True),
    )(send)


def gather_body(recv_ref, force_ref, coupling_ref, stiff_ref, faces_ref, first_ref, total):
    total[...] = jnp.zeros_like(total)
    lines = iota((256, 256), 0)
    places = iota((NP, 256), 0)
    zero = jnp.zeros((), BF16)

    def add(g, carry):
        lhs, rhs = [], []
        for h in range(2):
            code = recv_ref[g, 4 * h + 3 : 4 * h + 4, :].astype(I32)
            hit = places == (code >> 8)
            parts = []
            for c in range(3):
                for part in split(recv_ref[g, 4 * h + c : 4 * h + c + 1, :]):
                    parts.append(jnp.where(hit, jnp.broadcast_to(part, (NP, 256)), zero))
            lhs.append(jnp.concatenate(parts, axis=0))
            rhs.append(jnp.where(lines == (code & 255), 1.0, 0.0).astype(BF16))
        total[...] += lax.dot_general(
            jnp.concatenate(lhs, axis=1), jnp.concatenate(rhs, axis=1), NT, preferred_element_type=F32
        )
        return carry

    lax.fori_loop(0, GROUPS, add, 0)
    diagonal = stiff_ref[...] + jnp.sum(coupling_ref[...], axis=0, keepdims=True)
    row = iota((8, 128), 0)
    first = jnp.zeros((8, 128), F32)
    for c in range(3):
        sums = total[2 * c * NP : (2 * c + 1) * NP, :] + total[(2 * c + 1) * NP : (2 * c + 2) * NP, :]
        load = jnp.sum(sums, axis=0, keepdims=True)
        load = load[:, 0:128] + load[:, 128:256]
        load = load + pltpu.roll(load, 64, axis=1)
        value = (force_ref[c : c + 1, :] + 0.25 * load[:, 0:64]) / diagonal
        first = jnp.where(row == c, jnp.concatenate([value, value], axis=1), first)
        full = jnp.concatenate([sums, jnp.zeros((128 - NP, 256), F32)], axis=0)
        faces_ref[c] = full.T
    first_ref[...] = first


def add_up(recv, force, coupling, stiff):
    return pl.pallas_call(
        gather_body,
        name="add_up",
        out_shape=(
            jax.ShapeDtypeStruct((3, 256, 128), F32),
            jax.ShapeDtypeStruct((8, 128), F32),
        ),
        in_specs=[VMEM_SPEC] * 4,
        out_specs=(VMEM_SPEC, VMEM_SPEC),
        scratch_shapes=[pltpu.VMEM((6 * NP, 256), F32)],
        compiler_params=pltpu.CompilerParams(vmem_limit_bytes=48 << 20),
    )(recv, force, coupling, stiff)


ROUNDS = 3


def sweep_body(
    first_ref, coupling_ref, stiff_ref, edges_ref, faces_ref,
    skel_ref, low_ref, high_ref,
    static, low_in, high_in, face_out, near, far, picks, weights,
    near_send, near_recv, far_send, far_recv, halo_send, halo_recv,
):
    g, s = lax.axis_index("group"), lax.axis_index("span")
    barrier = pltpu.get_barrier_semaphore()

    def greet_group(k, carry):
        pl.semaphore_signal(barrier, inc=1, device_id=((g + k) % GROUPS, s), device_id_type=MESH)
        return carry

    def greet_span(k, carry):
        pl.semaphore_signal(barrier, inc=1, device_id=(g, (s + k) % SPANS), device_id_type=MESH)
        return carry

    lax.fori_loop(1, GROUPS, greet_group, 0)
    lax.fori_loop(1, SPANS, greet_span, 0)

    lane = iota((8, 128), 1)
    own_half = lane < 64
    diagonal = stiff_ref[...] + jnp.sum(coupling_ref[...], axis=0, keepdims=True)
    share = coupling_ref[...] / diagonal
    blank = jnp.zeros((6, 64), F32)
    static[0:6, :] = jnp.concatenate([share, blank], axis=1)
    static[8:14, :] = jnp.concatenate([edges_ref[...].astype(F32), blank], axis=1)
    static[16:24, :] = first_ref[...]
    for c in range(3):
        face_out[0, c] = faces_ref[c, pl.ds(7, 32, stride=8), :]
        face_out[1, c] = faces_ref[c, pl.ds(0, 32, stride=8), :]

    def place(state):
        state = jnp.where(own_half, state, 0.0)
        return jnp.where(g % 2 == 1, pltpu.roll(state, 64, axis=1), state)[0:4, :]

    near[0, g] = place(first_ref[...])
    pl.semaphore_wait(barrier, GROUPS - 1 + SPANS - 1)

    def push_near(r):
        def push(k, carry):
            peer = (g + k) % GROUPS
            pltpu.make_async_remote_copy(
                near.at[r, g], near.at[r, g], near_send.at[r], near_recv.at[r],
                device_id=(peer, s), device_id_type=MESH,
            ).start()
            return carry

        lax.fori_loop(1, GROUPS, push, 0)

    push_near(0)
    up, down = (s + 1) % SPANS, (s + SPANS - 1) % SPANS
    halos = [
        pltpu.make_async_remote_copy(
            src, dst, halo_send.at[n], halo_recv.at[n], device_id=(g, to), device_id_type=MESH
        )
        for n, (src, dst, to) in enumerate(
            [
                (static, low_in, up),
                (static, high_in, down),
                (face_out.at[0], low_ref, up),
                (face_out.at[1], high_ref, down),
            ]
        )
    ]
    for halo in halos:
        halo.start()
    halos[0].wait_recv()
    halos[1].wait_recv()
    turn = lane & 7

    def extended(rows):
        beyond = jnp.where(turn == 7, low_in[rows, :], jnp.where(turn == 0, high_in[rows, :], 0.0))
        return jnp.where(own_half, static[rows, :], pltpu.roll(beyond, 64, axis=1))

    share = extended(slice(0, 8))
    edges = extended(slice(8, 16)).astype(I32)
    first = extended(slice(16, 24))
    for d in range(6):
        node = edges[d : d + 1, :]
        group, span, local = node >> 9, (node >> 6) & 7, node & 63
        column = (group & 1) * 64 + local
        pick = jnp.where(iota((128, 128), 0) == column, 1.0, 0.0).astype(BF16)
        cols = slice(d * 128, (d + 1) * 128)
        picks[0:128, cols] = pick
        picks[128:256, cols] = pick
        line = span * 16 + (group >> 1)
        weights[:, cols] = jnp.where(iota((128, 128), 0) == line, share[d : d + 1, :], 0.0)
    row = iota((8, 128), 0)
    state = first
    for r in range(ROUNDS):
        wait_for(near.at[r, pl.ds(0, GROUPS - 1)], near_recv.at[r])
        for h in range(16):
            pair = near[r, 2 * h] + near[r, 2 * h + 1]
            for c in range(3):
                far[r, s, c * 16 + h : c * 16 + h + 1, :] = pair[c : c + 1, :]

        def push(k, carry):
            peer = (s + k) % SPANS
            pltpu.make_async_remote_copy(
                far.at[r, s], far.at[r, s], far_send.at[r], far_recv.at[r],
                device_id=(g, peer), device_id_type=MESH,
            ).start()
            return carry

        lax.fori_loop(1, SPANS, push, 0)
        wait_for(far.at[r, pl.ds(0, SPANS - 1)], far_recv.at[r])
        table = far[r].reshape(SPANS * 48, 128)
        found = jnp.dot(jnp.concatenate(split(table), axis=1), picks[...], preferred_element_type=F32)
        found = found.reshape(SPANS, 3, 16, 768)
        weighted = weights[...].reshape(SPANS, 16, 768)
        state = first
        for c in range(3):
            total = jnp.sum((found[:, c] * weighted).reshape(SPANS * 16, 768), axis=0, keepdims=True)
            parts = [total[:, d * 128 : (d + 1) * 128] for d in range(6)]
            state = state + jnp.where(row == c, functools.reduce(jnp.add, parts), 0.0)
        if r + 1 < ROUNDS:
            near[r + 1, g] = place(state)
            push_near(r + 1)
    skel_ref[...] = state
    halos[2].wait_recv()
    halos[3].wait_recv()
    for halo in halos:
        halo.wait_send()
    for r in range(ROUNDS):
        wait_for(near.at[r, pl.ds(0, GROUPS - 1)], near_send.at[r])
        wait_for(far.at[r, pl.ds(0, SPANS - 1)], far_send.at[r])


def sweeps(first, coupling, stiff, edges, faces):
    dma = pltpu.SemaphoreType.DMA
    return pl.pallas_call(
        sweep_body,
        name="sweeps",
        out_shape=(
            jax.ShapeDtypeStruct((8, 128), F32),
            jax.ShapeDtypeStruct((3, 32, 128), F32),
            jax.ShapeDtypeStruct((3, 32, 128), F32),
        ),
        in_specs=[VMEM_SPEC] * 5,
        out_specs=(VMEM_SPEC,) * 3,
        scratch_shapes=[
            pltpu.VMEM((24, 128), F32),
            pltpu.VMEM((24, 128), F32),
            pltpu.VMEM((24, 128), F32),
            pltpu.VMEM((2, 3, 32, 128), F32),
            pltpu.VMEM((ROUNDS, GROUPS, 4, 128), F32),
            pltpu.VMEM((ROUNDS, SPANS, 48, 128), F32),
            pltpu.VMEM((256, 768), BF16),
            pltpu.VMEM((128, 768), F32),
            dma((ROUNDS,)), dma((ROUNDS,)), dma((ROUNDS,)), dma((ROUNDS,)), dma((4,)), dma((4,)),
        ],
        compiler_params=pltpu.CompilerParams(
            collective_id=1, has_side_effects=True, vmem_limit_bytes=48 << 20
        ),
    )(first, coupling, stiff, edges, faces)


def blend_tables():
    f = np.arange(NP * NP)
    i, j = f % NP, f // NP
    n = NP - 1
    s, t = i / n, j / n

    def bubble(i, j):
        s, t = i / n, j / n
        return 16.0 * s * (1 - s) * t * (1 - t)

    ip, im = np.minimum(i + 1, n), np.maximum(i - 1, 0)
    jp, jm = np.minimum(j + 1, n), np.maximum(j - 1, 0)
    rows = [
        s, t, (ip - im) / (2.0 * n), (jp - jm) / (2.0 * n),
        bubble(i, j), 0.5 * (bubble(ip, j) - bubble(im, j)), 0.5 * (bubble(i, jp) - bubble(i, jm)),
    ]
    rows.append(np.zeros_like(s))
    return np.stack(rows).astype(np.float32), np.stack([i, j] + [i] * 6).astype(np.int32)


def pick_lanes(x, index):
    return jnp.take_along_axis(x, index, axis=1)


def blend_body(spacing_ref, faces_ref, low_ref, high_ref, skel_ref, table_ref, index_ref, disp_ref, jac_ref):
    q = pl.program_id(0)
    span = lax.axis_index("span")
    has_low = jnp.where(span > 0, 1.0, 0.0).astype(F32)
    has_high = jnp.where(span < SPANS - 1, 1.0, 0.0).astype(F32)
    row, lane = iota((8, 128), 0), iota((8, 128), 1)
    frac = lane.astype(F32) * (1.0 / (NP - 1))

    def along_span(x, before, after):
        nxt = jnp.where(row == 7, after * has_high, pltpu.roll(x, 7, axis=0))
        prv = jnp.where(row == 0, before * has_low, pltpu.roll(x, 1, axis=0))
        return 0.5 * (nxt - prv)

    def along_lane(x):
        nxt = jnp.where(lane == NP - 1, x, pltpu.roll(x, 127, axis=1))
        prv = jnp.where(lane == 0, x, pltpu.roll(x, 1, axis=1))
        return 0.5 * (nxt - prv)

    def inner(x):
        return x - (1.0 - frac) * x[:, 0:1] - frac * x[:, NP - 1 : NP]

    lane_fns, column_fns, bumps = [], [], []
    for c in range(3):
        now, diff = [], []
        for seg in range(4):
            x = faces_ref[c, pl.ds(pl.multiple_of(seg * LAYERS + q * 8, 8), 8), :]
            before = low_ref[c, pl.ds(seg * 8 + q, 1), :]
            after = high_ref[c, pl.ds(seg * 8 + q, 1), :]
            now.append(x)
            diff.append(along_span(x, before, after))
        values = []
        for bottom, top, left, right in (now, diff):
            base = inner(bottom)
            values.append((base, inner(top) - base, left, right - left))
        (b, d, left, m), (b_s, d_s, left_s, m_s) = values
        lane_fns.append((b, d, along_lane(b), along_lane(d), b_s, d_s))
        column_fns.append((left, m, along_lane(left), along_lane(m), left_s, m_s))
        skel = jnp.broadcast_to(skel_ref[c : c + 1, :], (8, 128))

        def column(where):
            return jnp.sum(jnp.where(where, skel, 0.0), axis=1, keepdims=True)

        value = column(lane == q * 8 + row)
        nxt = column(lane == jnp.where(row == 7, 64 + q * 8, q * 8 + row + 1))
        prv = column(lane == jnp.where(row == 0, 64 + q * 8 + 7, q * 8 + row - 1))
        nxt = jnp.where(row == 7, nxt * has_high, nxt)
        prv = jnp.where(row == 0, prv * has_low, prv)
        bumps.append((jnp.broadcast_to(value, (8, 128)), 0.5 * (nxt - prv)))
    spacing = [spacing_ref[c, q] for c in range(3)]

    for phase in range(5):
        where = jnp.broadcast_to(index_ref[0:1, phase * 128 : (phase + 1) * 128], (8, 128))
        lanes = [[pick_lanes(x, where) for x in fns] for fns in lane_fns]
        for turn in range(10):
            cols = slice((turn * 5 + phase) * 128, (turn * 5 + phase + 1) * 128)
            where = jnp.broadcast_to(index_ref[1:2, cols], (8, 128))
            s, t, s_i, t_j, bump, bump_i, bump_j = [table_ref[n : n + 1, cols] for n in range(7)]
            matrix = []
            for c in range(3):
                b, d, b_i, d_i, b_s, d_s = lanes[c]
                left, m, left_j, m_j, left_s, m_s = [pick_lanes(x, where) for x in column_fns[c]]
                k, k_s = bumps[c]
                disp_ref[c, 0, :, cols] = b + t * d + left + s * m + bump * k
                matrix.append(
                    [
                        b_i + t * d_i + s_i * m + bump_i * k,
                        t_j * d + left_j + s * m_j + bump_j * k,
                        b_s + t * d_s + left_s + s * m_s + bump * k_s,
                    ]
                )
                matrix[c][c] = matrix[c][c] + spacing[c]
            one = matrix[1][1] * matrix[2][2] - matrix[1][2] * matrix[2][1]
            two = matrix[1][0] * matrix[2][2] - matrix[1][2] * matrix[2][0]
            three = matrix[1][0] * matrix[2][1] - matrix[1][1] * matrix[2][0]
            jac_ref[0, :, cols] = matrix[0][0] * one - matrix[0][1] * two + matrix[0][2] * three


def blend(spacing, faces, low, high, skel):
    table, index = blend_tables()
    whole = lambda *shape: pl.BlockSpec(shape, lambda q: (0,) * len(shape))
    return pl.pallas_call(
        blend_body,
        name="blend",
        grid=(8,),
        out_shape=(
            jax.ShapeDtypeStruct((3, 8, 8, NP * NP), F32),
            jax.ShapeDtypeStruct((8, 8, NP * NP), F32),
        ),
        in_specs=[
            pl.BlockSpec(memory_space=pltpu.SMEM),
            whole(3, 256, 128),
            whole(3, 32, 128),
            whole(3, 32, 128),
            whole(8, 128),
            whole(8, NP * NP),
            whole(8, NP * NP),
        ],
        out_specs=(
            pl.BlockSpec((3, 1, 8, NP * NP), lambda q: (0, q, 0, 0)),
            pl.BlockSpec((1, 8, NP * NP), lambda q: (q, 0, 0)),
        ),
        compiler_params=pltpu.CompilerParams(
            dimension_semantics=("arbitrary",), vmem_limit_bytes=48 << 20
        ),
    )(spacing, faces, low, high, skel, jnp.asarray(table), jnp.asarray(index))


def on_device(disp, weight, owner, row, force, coupling, stiff, edges, spacing):
    stiff = stiff.reshape(1, -1)
    send = pack(disp, weight.T, owner.T, row.T)
    recv = exchange(send)
    faces, first = add_up(recv, force, coupling, stiff)
    skel, low, high = sweeps(first, coupling, stiff, edges, faces)
    return blend(spacing, faces, low, high, skel)


def solution(mesh):
    return jax.shard_map(
        on_device,
        mesh=mesh,
        in_specs=(
            P(None, ("group", "span")),
            P(("group", "span"), None),
            P(("group", "span"), None),
            P(("group", "span"), None),
            P(None, ("group", "span")),
            P(None, ("group", "span")),
            P(("group", "span")),
            P(None, ("group", "span")),
            P(None, "group"),
        ),
        out_specs=(P(None, "group", "span", None), P("group", "span", None)),
        check_vma=False,
    )
```

```python
import functools

import jax
import jax.numpy as jnp
import numpy as np
from jax import lax
from jax.experimental import pallas as pl
from jax.experimental.pallas import tpu as pltpu
from jax.sharding import PartitionSpec as P

F32, BF16, I32 = jnp.float32, jnp.bfloat16, jnp.int32
NP = 80
LAYERS = 64
GROUPS, SPANS = 32, 8
NODES = 2048
MESH = pl.DeviceIdType.MESH
NT = (((1,), (1,)), ((), ()))
VMEM_SPEC = pl.BlockSpec(memory_space=pltpu.VMEM)


def iota(shape, dim):
    return lax.broadcasted_iota(I32, shape, dim)


def split(value):
    high = value.astype(BF16)
    return high, (value - high.astype(F32)).astype(BF16)


def wait_for(ref, sem):
    pltpu.make_async_copy(ref, ref, sem).wait()


def offset_peer(g, k):
    n, m = k // 4, k % 4
    dz = 4 + ((n + 1) // 2) * (1 - 2 * (n % 2))
    dx = 2 + ((m + 1) // 2) * (1 - 2 * (m % 2))
    return ((g // 8 + dx) % 4) * 8 + (g % 8 + dz) % 8


def pack(disp_ref, weight_ref, owner_ref, row_ref, out_ref, lhs, rhs):
    group_rows = iota((GROUPS, NODES), 0)
    present = jnp.zeros((GROUPS, NODES), F32)
    for t in range(4):
        present += jnp.where(owner_ref[t : t + 1, :] == group_rows, 1.0, 0.0)
    present = present.astype(BF16)
    before = jnp.where(iota((256, 256), 0) < iota((256, 256), 1), 1.0, 0.0).astype(BF16)
    every = jnp.ones((256, 256), BF16)
    base = jnp.zeros((GROUPS, 256), F32)
    ranks = []
    for k in range(NODES // 256):
        piece = present[:, k * 256 : (k + 1) * 256]
        ranks.append(jnp.dot(piece, before, preferred_element_type=F32) + base)
        base += jnp.dot(piece, every, preferred_element_type=F32)
    rank = jnp.concatenate(ranks, axis=1)
    word = iota((8, NODES), 0) & 3
    total = jnp.zeros((512, 256), F32)
    for t in range(4):
        owner = owner_ref[t : t + 1, :]
        slot = jnp.sum(jnp.where(owner == group_rows, rank, 0.0), axis=0, keepdims=True).astype(I32)
        half = slot >> 8
        column = slot & 255
        bucket = owner * 2 + half
        row = row_ref[t : t + 1, :]
        layer = ((row >> 6) * 205) >> 10
        edge = row - layer * (4 * NP)
        seg = ((edge >> 4) * 205) >> 10
        along = (edge - seg * NP) << 8
        line = seg * LAYERS + layer
        weight = weight_ref[t : t + 1, :]
        value = jnp.where(
            word == 0, disp_ref[0:1, :], jnp.where(word == 1, disp_ref[1:2, :], disp_ref[2:3, :])
        ) * weight
        high = jnp.where(word == 3, along.astype(F32), value).astype(BF16)
        low = jnp.where(word == 3, line.astype(F32), value - high.astype(F32)).astype(BF16)
        high = jnp.concatenate([high] * 32, axis=0)
        low = jnp.concatenate([low] * 32, axis=0)
        hit = (iota((256, NODES), 0) >> 2) == bucket
        zero = jnp.zeros((), BF16)
        lhs[0:256, :] = jnp.where(hit, high, zero)
        lhs[256:512, :] = jnp.where(hit, low, zero)
        rhs[...] = jnp.where(iota((256, NODES), 0) == column, 1.0, 0.0).astype(BF16)
        total += lax.dot_general(lhs[...], rhs[...], NT, preferred_element_type=F32)
    out_ref[...] = (total[0:256] + total[256:512]).reshape(GROUPS, 8, 256)


def add_up(recv_ref, sources):
    lines = iota((256, 256), 0)
    places = iota((NP, 256), 0)
    zero = jnp.zeros((), BF16)
    lhs, rhs = [], []
    for source in sources:
        for h in range(2):
            code = recv_ref[source, 4 * h + 3 : 4 * h + 4, :].astype(I32)
            hit = places == (code >> 8)
            parts = []
            for c in range(3):
                for part in split(recv_ref[source, 4 * h + c : 4 * h + c + 1, :]):
                    parts.append(jnp.where(hit, jnp.broadcast_to(part, (NP, 256)), zero))
            lhs.append(jnp.concatenate(parts, axis=0))
            rhs.append(jnp.where(lines == (code & 255), 1.0, 0.0).astype(BF16))
    return lax.dot_general(
        jnp.concatenate(lhs, axis=1), jnp.concatenate(rhs, axis=1), NT, preferred_element_type=F32
    )


ROUNDS = 3
TOGETHER = 4


def front_body(
    disp_hbm, weight_hbm, owner_hbm, row_hbm, force_hbm, coupling_hbm, stiff_hbm, edges_hbm,
    faces_ref, skel_ref, low_ref, high_ref,
    disp_ref, weight_ref, owner_ref, row_ref, force_ref, coupling_ref, stiff_ref, edges_ref,
    lhs, rhs, send, recv, total, first_ref, first_low, first_high,
    static, low_in, high_in, face_out, near, far, picks, weights,
    load_sem, send_sem, recv_sem, near_send, near_recv, far_send, far_recv, halo_send, halo_recv,
):
    g, s = lax.axis_index("group"), lax.axis_index("span")
    up, down = (s + 1) % SPANS, (s + SPANS - 1) % SPANS
    loads = [
        pltpu.make_async_copy(src, dst, load_sem.at[n])
        for n, (src, dst) in enumerate(
            [
                (owner_hbm, owner_ref), (row_hbm, row_ref), (disp_hbm, disp_ref), (weight_hbm, weight_ref),
                (coupling_hbm, coupling_ref), (stiff_hbm, stiff_ref), (edges_hbm, edges_ref), (force_hbm, force_ref),
            ]
        )
    ]
    for load in loads:
        load.start()
    barrier = pltpu.get_barrier_semaphore()

    def greet_group(k, carry):
        pl.semaphore_signal(barrier, inc=1, device_id=(offset_peer(g, k), s), device_id_type=MESH)
        return carry

    def greet_span(k, carry):
        pl.semaphore_signal(barrier, inc=1, device_id=(g, (s + k) % SPANS), device_id_type=MESH)
        return carry

    lax.fori_loop(0, GROUPS - 1, greet_group, 0)
    lax.fori_loop(1, SPANS, greet_span, 0)
    for load in loads:
        load.wait()
    pack(disp_ref, weight_ref, owner_ref, row_ref, send, lhs, rhs)
    recv[g] = send[g]
    diagonal = stiff_ref[...] + jnp.sum(coupling_ref[...], axis=0, keepdims=True)
    blank = jnp.zeros((6, 64), F32)
    static[0:6, :] = jnp.concatenate([coupling_ref[...] / diagonal, blank], axis=1)
    static[8:14, :] = jnp.concatenate([edges_ref[...].astype(F32), blank], axis=1)
    pl.semaphore_wait(barrier, GROUPS - 1 + SPANS - 1)

    def push_send(k, carry):
        peer = offset_peer(g, k)
        pltpu.make_async_remote_copy(
            send.at[peer], recv.at[g], send_sem, recv_sem.at[g], device_id=(peer, s), device_id_type=MESH
        ).start()
        return carry

    lax.fori_loop(0, GROUPS - 1, push_send, 0)
    halos = [
        pltpu.make_async_remote_copy(
            src, dst, halo_send.at[n], halo_recv.at[n], device_id=(g, to), device_id_type=MESH
        )
        for n, (src, dst, to) in enumerate(
            [
                (static, low_in, up), (static, high_in, down),
                (first_ref, first_low, up), (first_ref, first_high, down),
                (face_out.at[0], low_ref, up), (face_out.at[1], high_ref, down),
            ]
        )
    ]
    halos[0].start()
    halos[1].start()
    total[...] = add_up(recv, [g])
    halos[0].wait_recv()
    halos[1].wait_recv()
    lane = iota((8, 128), 1)
    own_half, turn = lane < 64, lane & 7

    def extended(own, below, above):
        beyond = jnp.where(turn == 7, below, jnp.where(turn == 0, above, 0.0))
        return jnp.where(own_half, own, pltpu.roll(beyond, 64, axis=1))

    share, edges = [
        extended(static[rows, :], low_in[rows, :], high_in[rows, :]) for rows in (slice(0, 8), slice(8, 16))
    ]
    edges = edges.astype(I32)
    for d in range(6):
        node = edges[d : d + 1, :]
        group, span, local = node >> 9, (node >> 6) & 7, node & 63
        column = (group & 1) * 64 + local
        pick = jnp.where(iota((128, 128), 0) == column, 1.0, 0.0).astype(BF16)
        cols = slice(d * 128, (d + 1) * 128)
        picks[0:128, cols] = pick
        picks[128:256, cols] = pick
        line = span * 16 + (group >> 1)
        weights[:, cols] = jnp.where(iota((128, 128), 0) == line, share[d : d + 1, :], 0.0)

    for k in range(GROUPS - 2, -1, -TOGETHER):
        sources = [offset_peer(g, n) for n in range(k, max(k - TOGETHER, -1), -1)]
        for source in sources:
            wait_for(recv.at[source], recv_sem.at[source])
        total[...] += add_up(recv, sources)

    row = iota((8, 128), 0)
    first = jnp.zeros((8, 128), F32)
    for c in range(3):
        sums = total[2 * c * NP : (2 * c + 1) * NP, :] + total[(2 * c + 1) * NP : (2 * c + 2) * NP, :]
        load = jnp.sum(sums, axis=0, keepdims=True)
        load = load[:, 0:128] + load[:, 128:256]
        load = load + pltpu.roll(load, 64, axis=1)
        value = (force_ref[c : c + 1, :] + 0.25 * load[:, 0:64]) / diagonal
        first = jnp.where(row == c, jnp.concatenate([value, value], axis=1), first)
        total[2 * c * NP : (2 * c + 1) * NP, :] = sums
    first_ref[...] = first

    def place(state):
        state = jnp.where(own_half, state, 0.0)
        return jnp.where(g % 2 == 1, pltpu.roll(state, 64, axis=1), state)[0:4, :]

    def push_near(r):
        def push(k, carry):
            pltpu.make_async_remote_copy(
                near.at[r, g], near.at[r, g], near_send.at[r], near_recv.at[r],
                device_id=(offset_peer(g, k), s), device_id_type=MESH,
            ).start()
            return carry

        lax.fori_loop(0, GROUPS - 1, push, 0)

    near[0, g] = place(first)
    push_near(0)
    halos[2].start()
    halos[3].start()
    for c in range(3):
        full = jnp.concatenate([total[2 * c * NP : (2 * c + 1) * NP, :], jnp.zeros((128 - NP, 256), F32)], axis=0)
        faces_ref[c] = full.T
    for c in range(3):
        face_out[0, c] = faces_ref[c, pl.ds(7, 32, stride=8), :]
        face_out[1, c] = faces_ref[c, pl.ds(0, 32, stride=8), :]
    halos[4].start()
    halos[5].start()
    halos[2].wait_recv()
    halos[3].wait_recv()
    first = extended(first, first_low[...], first_high[...])
    state = first
    for r in range(ROUNDS):
        wait_for(near.at[r, pl.ds(0, GROUPS - 1)], near_recv.at[r])
        for h in range(16):
            pair = near[r, 2 * h] + near[r, 2 * h + 1]
            for c in range(3):
                far[r, s, c * 16 + h : c * 16 + h + 1, :] = pair[c : c + 1, :]

        def push(k, carry):
            peer = (s + k) % SPANS
            pltpu.make_async_remote_copy(
                far.at[r, s], far.at[r, s], far_send.at[r], far_recv.at[r],
                device_id=(g, peer), device_id_type=MESH,
            ).start()
            return carry

        lax.fori_loop(1, SPANS, push, 0)
        wait_for(far.at[r, pl.ds(0, SPANS - 1)], far_recv.at[r])
        table = far[r].reshape(SPANS * 48, 128)
        found = jnp.dot(jnp.concatenate(split(table), axis=1), picks[...], preferred_element_type=F32)
        found = found.reshape(SPANS, 3, 16, 768)
        weighted = weights[...].reshape(SPANS, 16, 768)
        state = first
        for c in range(3):
            sums = jnp.sum((found[:, c] * weighted).reshape(SPANS * 16, 768), axis=0, keepdims=True)
            parts = [sums[:, d * 128 : (d + 1) * 128] for d in range(6)]
            state = state + jnp.where(row == c, functools.reduce(jnp.add, parts), 0.0)
        if r + 1 < ROUNDS:
            near[r + 1, g] = place(state)
            push_near(r + 1)
    skel_ref[...] = state
    halos[4].wait_recv()
    halos[5].wait_recv()
    wait_for(send.at[pl.ds(0, GROUPS - 1)], send_sem)
    for halo in halos:
        halo.wait_send()
    for r in range(ROUNDS):
        wait_for(near.at[r, pl.ds(0, GROUPS - 1)], near_send.at[r])
        wait_for(far.at[r, pl.ds(0, SPANS - 1)], far_send.at[r])


def front(disp, weight, owner, row, force, coupling, stiff, edges):
    dma = pltpu.SemaphoreType.DMA
    local = [pltpu.VMEM(x.shape, x.dtype) for x in (disp, weight, owner, row, force, coupling, stiff, edges)]
    return pl.pallas_call(
        front_body,
        name="front",
        out_shape=(
            jax.ShapeDtypeStruct((3, 256, 128), F32),
            jax.ShapeDtypeStruct((8, 128), F32),
            jax.ShapeDtypeStruct((3, 32, 128), F32),
            jax.ShapeDtypeStruct((3, 32, 128), F32),
        ),
        in_specs=[pl.BlockSpec(memory_space=pltpu.HBM)] * 8,
        out_specs=(VMEM_SPEC,) * 4,
        scratch_shapes=[
            *local,
            pltpu.VMEM((512, NODES), BF16), pltpu.VMEM((256, NODES), BF16),
            pltpu.VMEM((GROUPS, 8, 256), F32), pltpu.VMEM((GROUPS, 8, 256), F32),
            pltpu.VMEM((6 * NP, 256), F32),
            pltpu.VMEM((8, 128), F32), pltpu.VMEM((8, 128), F32), pltpu.VMEM((8, 128), F32),
            pltpu.VMEM((16, 128), F32), pltpu.VMEM((16, 128), F32), pltpu.VMEM((16, 128), F32),
            pltpu.VMEM((2, 3, 32, 128), F32),
            pltpu.VMEM((ROUNDS, GROUPS, 4, 128), F32),
            pltpu.VMEM((ROUNDS, SPANS, 48, 128), F32),
            pltpu.VMEM((256, 768), BF16),
            pltpu.VMEM((128, 768), F32),
            dma((8,)), dma, dma((GROUPS,)),
            dma((ROUNDS,)), dma((ROUNDS,)), dma((ROUNDS,)), dma((ROUNDS,)), dma((6,)), dma((6,)),
        ],
        compiler_params=pltpu.CompilerParams(
            collective_id=0, has_side_effects=True, vmem_limit_bytes=48 << 20
        ),
    )(disp, weight, owner, row, force, coupling, stiff, edges)


def blend_tables():
    f = np.arange(NP * NP)
    i, j = f % NP, f // NP
    n = NP - 1
    s, t = i / n, j / n

    def bubble(i, j):
        s, t = i / n, j / n
        return 16.0 * s * (1 - s) * t * (1 - t)

    ip, im = np.minimum(i + 1, n), np.maximum(i - 1, 0)
    jp, jm = np.minimum(j + 1, n), np.maximum(j - 1, 0)
    rows = [
        s, t, (ip - im) / (2.0 * n), (jp - jm) / (2.0 * n),
        bubble(i, j), 0.5 * (bubble(ip, j) - bubble(im, j)), 0.5 * (bubble(i, jp) - bubble(i, jm)),
    ]
    rows.append(np.zeros_like(s))
    return np.stack(rows).astype(np.float32), np.stack([i, j] + [i] * 6).astype(np.int32)


def pick_lanes(x, index):
    return jnp.take_along_axis(x, index, axis=1)


def blend_body(spacing_ref, faces_ref, low_ref, high_ref, skel_ref, table_ref, index_ref, disp_ref, jac_ref):
    q = pl.program_id(0)
    span = lax.axis_index("span")
    has_low = jnp.where(span > 0, 1.0, 0.0).astype(F32)
    has_high = jnp.where(span < SPANS - 1, 1.0, 0.0).astype(F32)
    row, lane = iota((8, 128), 0), iota((8, 128), 1)
    frac = lane.astype(F32) * (1.0 / (NP - 1))

    def along_span(x, before, after):
        nxt = jnp.where(row == 7, after * has_high, pltpu.roll(x, 7, axis=0))
        prv = jnp.where(row == 0, before * has_low, pltpu.roll(x, 1, axis=0))
        return 0.5 * (nxt - prv)

    def along_lane(x):
        nxt = jnp.where(lane == NP - 1, x, pltpu.roll(x, 127, axis=1))
        prv = jnp.where(lane == 0, x, pltpu.roll(x, 1, axis=1))
        return 0.5 * (nxt - prv)

    def inner(x):
        return x - (1.0 - frac) * x[:, 0:1] - frac * x[:, NP - 1 : NP]

    lane_fns, column_fns, bumps = [], [], []
    for c in range(3):
        now, diff = [], []
        for seg in range(4):
            x = faces_ref[c, pl.ds(pl.multiple_of(seg * LAYERS + q * 8, 8), 8), :]
            before = low_ref[c, pl.ds(seg * 8 + q, 1), :]
            after = high_ref[c, pl.ds(seg * 8 + q, 1), :]
            now.append(x)
            diff.append(along_span(x, before, after))
        values = []
        for bottom, top, left, right in (now, diff):
            base = inner(bottom)
            values.append((base, inner(top) - base, left, right - left))
        (b, d, left, m), (b_s, d_s, left_s, m_s) = values
        lane_fns.append((b, d, along_lane(b), along_lane(d), b_s, d_s))
        column_fns.append((left, m, along_lane(left), along_lane(m), left_s, m_s))
        skel = jnp.broadcast_to(skel_ref[c : c + 1, :], (8, 128))

        def column(where):
            return jnp.sum(jnp.where(where, skel, 0.0), axis=1, keepdims=True)

        value = column(lane == q * 8 + row)
        nxt = column(lane == jnp.where(row == 7, 64 + q * 8, q * 8 + row + 1))
        prv = column(lane == jnp.where(row == 0, 64 + q * 8 + 7, q * 8 + row - 1))
        nxt = jnp.where(row == 7, nxt * has_high, nxt)
        prv = jnp.where(row == 0, prv * has_low, prv)
        bumps.append((jnp.broadcast_to(value, (8, 128)), 0.5 * (nxt - prv)))
    spacing = [spacing_ref[c, q] for c in range(3)]

    for phase in range(5):
        where = jnp.broadcast_to(index_ref[0:1, phase * 128 : (phase + 1) * 128], (8, 128))
        lanes = [[pick_lanes(x, where) for x in fns] for fns in lane_fns]
        for turn in range(10):
            cols = slice((turn * 5 + phase) * 128, (turn * 5 + phase + 1) * 128)
            where = jnp.broadcast_to(index_ref[1:2, cols], (8, 128))
            s, t, s_i, t_j, bump, bump_i, bump_j = [table_ref[n : n + 1, cols] for n in range(7)]
            matrix = []
            for c in range(3):
                b, d, b_i, d_i, b_s, d_s = lanes[c]
                left, m, left_j, m_j, left_s, m_s = [pick_lanes(x, where) for x in column_fns[c]]
                k, k_s = bumps[c]
                disp_ref[c, 0, :, cols] = b + t * d + left + s * m + bump * k
                matrix.append(
                    [
                        b_i + t * d_i + s_i * m + bump_i * k,
                        t_j * d + left_j + s * m_j + bump_j * k,
                        b_s + t * d_s + left_s + s * m_s + bump * k_s,
                    ]
                )
                matrix[c][c] = matrix[c][c] + spacing[c]
            one = matrix[1][1] * matrix[2][2] - matrix[1][2] * matrix[2][1]
            two = matrix[1][0] * matrix[2][2] - matrix[1][2] * matrix[2][0]
            three = matrix[1][0] * matrix[2][1] - matrix[1][1] * matrix[2][0]
            jac_ref[0, :, cols] = matrix[0][0] * one - matrix[0][1] * two + matrix[0][2] * three


def blend(spacing, faces, low, high, skel):
    table, index = blend_tables()
    whole = lambda *shape: pl.BlockSpec(shape, lambda q: (0,) * len(shape))
    return pl.pallas_call(
        blend_body,
        name="blend",
        grid=(8,),
        out_shape=(
            jax.ShapeDtypeStruct((3, 8, 8, NP * NP), F32),
            jax.ShapeDtypeStruct((8, 8, NP * NP), F32),
        ),
        in_specs=[
            pl.BlockSpec(memory_space=pltpu.SMEM),
            whole(3, 256, 128),
            whole(3, 32, 128),
            whole(3, 32, 128),
            whole(8, 128),
            whole(8, NP * NP),
            whole(8, NP * NP),
        ],
        out_specs=(
            pl.BlockSpec((3, 1, 8, NP * NP), lambda q: (0, q, 0, 0)),
            pl.BlockSpec((1, 8, NP * NP), lambda q: (q, 0, 0)),
        ),
        compiler_params=pltpu.CompilerParams(
            dimension_semantics=("arbitrary",), vmem_limit_bytes=48 << 20
        ),
    )(spacing, faces, low, high, skel, jnp.asarray(table), jnp.asarray(index))


def on_device(disp, weight, owner, row, force, coupling, stiff, edges, spacing):
    faces, skel, low, high = front(
        disp, weight.T, owner.T, row.T, force, coupling, stiff.reshape(1, -1), edges
    )
    return blend(spacing, faces, low, high, skel)


def solution(mesh):
    return jax.shard_map(
        on_device,
        mesh=mesh,
        in_specs=(
            P(None, ("group", "span")),
            P(("group", "span"), None),
            P(("group", "span"), None),
            P(("group", "span"), None),
            P(None, ("group", "span")),
            P(None, ("group", "span")),
            P(("group", "span")),
            P(None, ("group", "span")),
            P(None, "group"),
        ),
        out_specs=(P(None, "group", "span", None), P("group", "span", None)),
        check_vma=False,
    )
```

```python
import functools

import jax
import jax.numpy as jnp
import numpy as np
from jax import lax
from jax.experimental import pallas as pl
from jax.experimental.pallas import tpu as pltpu
from jax.sharding import PartitionSpec as P

F32, BF16, I32 = jnp.float32, jnp.bfloat16, jnp.int32
NP = 80
LAYERS = 64
GROUPS, SPANS = 32, 8
NODES = 2048
MESH = pl.DeviceIdType.MESH
NT = (((1,), (1,)), ((), ()))
VMEM_SPEC = pl.BlockSpec(memory_space=pltpu.VMEM)


def iota(shape, dim):
    return lax.broadcasted_iota(I32, shape, dim)


def split(value):
    high = value.astype(BF16)
    return high, (value - high.astype(F32)).astype(BF16)


def wait_for(ref, sem):
    pltpu.make_async_copy(ref, ref, sem).wait()


def offset_peer(g, k):
    n, m = k // 4, k % 4
    dz = 4 + ((n + 1) // 2) * (1 - 2 * (n % 2))
    dx = 2 + ((m + 1) // 2) * (1 - 2 * (m % 2))
    return ((g // 8 + dx) % 4) * 8 + (g % 8 + dz) % 8


def pack(disp_ref, weight_ref, owner_ref, row_ref, out_ref, lhs, rhs):
    group_rows = iota((GROUPS, NODES), 0)
    present = jnp.zeros((GROUPS, NODES), F32)
    for t in range(4):
        present += jnp.where(owner_ref[t : t + 1, :] == group_rows, 1.0, 0.0)
    present = present.astype(BF16)
    before = jnp.where(iota((256, 256), 0) < iota((256, 256), 1), 1.0, 0.0).astype(BF16)
    every = jnp.ones((256, 256), BF16)
    base = jnp.zeros((GROUPS, 256), F32)
    ranks = []
    for k in range(NODES // 256):
        piece = present[:, k * 256 : (k + 1) * 256]
        ranks.append(jnp.dot(piece, before, preferred_element_type=F32) + base)
        base += jnp.dot(piece, every, preferred_element_type=F32)
    rank = jnp.concatenate(ranks, axis=1)
    word = iota((8, NODES), 0) & 3
    total = jnp.zeros((512, 256), F32)
    for t in range(4):
        owner = owner_ref[t : t + 1, :]
        slot = jnp.sum(jnp.where(owner == group_rows, rank, 0.0), axis=0, keepdims=True).astype(I32)
        half = slot >> 8
        column = slot & 255
        bucket = owner * 2 + half
        row = row_ref[t : t + 1, :]
        layer = ((row >> 6) * 205) >> 10
        edge = row - layer * (4 * NP)
        seg = ((edge >> 4) * 205) >> 10
        along = (edge - seg * NP) << 8
        line = seg * LAYERS + layer
        weight = weight_ref[t : t + 1, :]
        value = jnp.where(
            word == 0, disp_ref[0:1, :], jnp.where(word == 1, disp_ref[1:2, :], disp_ref[2:3, :])
        ) * weight
        high = jnp.where(word == 3, along.astype(F32), value).astype(BF16)
        low = jnp.where(word == 3, line.astype(F32), value - high.astype(F32)).astype(BF16)
        high = jnp.concatenate([high] * 32, axis=0)
        low = jnp.concatenate([low] * 32, axis=0)
        hit = (iota((256, NODES), 0) >> 2) == bucket
        zero = jnp.zeros((), BF16)
        lhs[0:256, :] = jnp.where(hit, high, zero)
        lhs[256:512, :] = jnp.where(hit, low, zero)
        rhs[...] = jnp.where(iota((256, NODES), 0) == column, 1.0, 0.0).astype(BF16)
        total += lax.dot_general(lhs[...], rhs[...], NT, preferred_element_type=F32)
    out_ref[...] = (total[0:256] + total[256:512]).reshape(GROUPS, 8, 256)


def add_up(recv_ref, sources):
    lines = iota((256, 256), 0)
    places = iota((NP, 256), 0)
    zero = jnp.zeros((), BF16)
    lhs, rhs = [], []
    for source in sources:
        for h in range(2):
            code = recv_ref[source, 4 * h + 3 : 4 * h + 4, :].astype(I32)
            hit = places == (code >> 8)
            parts = []
            for c in range(3):
                for part in split(recv_ref[source, 4 * h + c : 4 * h + c + 1, :]):
                    parts.append(jnp.where(hit, jnp.broadcast_to(part, (NP, 256)), zero))
            lhs.append(jnp.concatenate(parts, axis=0))
            rhs.append(jnp.where(lines == (code & 255), 1.0, 0.0).astype(BF16))
    return lax.dot_general(
        jnp.concatenate(lhs, axis=1), jnp.concatenate(rhs, axis=1), NT, preferred_element_type=F32
    )


ROUNDS = 2
TOGETHER = 4


def front_body(
    disp_hbm, weight_hbm, owner_hbm, row_hbm, force_hbm, coupling_hbm, stiff_hbm, edges_hbm,
    faces_ref, skel_ref, low_ref, high_ref,
    disp_ref, weight_ref, owner_ref, row_ref, force_ref, coupling_ref, stiff_ref, edges_ref,
    lhs, rhs, send, recv, total,
    static, low_in, high_in, face_out, near, far, picks, weights, near_rows, far_rows, picks2, weights2,
    load_sem, send_sem, recv_sem, near_send, near_recv, far_send, far_recv, halo_send, halo_recv,
    rows_send, rows_recv,
):
    g, s = lax.axis_index("group"), lax.axis_index("span")
    up, down = (s + 1) % SPANS, (s + SPANS - 1) % SPANS
    loads = [
        pltpu.make_async_copy(src, dst, load_sem.at[n])
        for n, (src, dst) in enumerate(
            [
                (owner_hbm, owner_ref), (row_hbm, row_ref), (disp_hbm, disp_ref), (weight_hbm, weight_ref),
                (coupling_hbm, coupling_ref), (stiff_hbm, stiff_ref), (edges_hbm, edges_ref), (force_hbm, force_ref),
            ]
        )
    ]
    for load in loads:
        load.start()
    barrier = pltpu.get_barrier_semaphore()

    def greet_group(k, carry):
        pl.semaphore_signal(barrier, inc=1, device_id=(offset_peer(g, k), s), device_id_type=MESH)
        return carry

    def greet_span(k, carry):
        pl.semaphore_signal(barrier, inc=1, device_id=(g, (s + k) % SPANS), device_id_type=MESH)
        return carry

    lax.fori_loop(0, GROUPS - 1, greet_group, 0)
    lax.fori_loop(1, SPANS, greet_span, 0)
    for load in loads:
        load.wait()
    pack(disp_ref, weight_ref, owner_ref, row_ref, send, lhs, rhs)
    recv[g] = send[g]
    diagonal = stiff_ref[...] + jnp.sum(coupling_ref[...], axis=0, keepdims=True)
    blank = jnp.zeros((6, 64), F32)
    static[0:6, :] = jnp.concatenate([coupling_ref[...] / diagonal, blank], axis=1)
    static[8:14, :] = jnp.concatenate([edges_ref[...].astype(F32), blank], axis=1)
    near_rows[g] = jnp.concatenate(
        [
            jnp.concatenate([coupling_ref[...] / diagonal, edges_ref[...].astype(F32)], axis=1),
            jnp.zeros((2, 128), F32),
        ],
        axis=0,
    )
    pl.semaphore_wait(barrier, GROUPS - 1 + SPANS - 1)

    def push_send(k, carry):
        peer = offset_peer(g, k)
        pltpu.make_async_remote_copy(
            send.at[peer], recv.at[g], send_sem, recv_sem.at[g], device_id=(peer, s), device_id_type=MESH
        ).start()
        return carry

    lax.fori_loop(0, GROUPS - 1, push_send, 0)
    halos = [
        pltpu.make_async_remote_copy(
            src, dst, halo_send.at[n], halo_recv.at[n], device_id=(g, to), device_id_type=MESH
        )
        for n, (src, dst, to) in enumerate(
            [
                (static, low_in, up), (static, high_in, down),
                (face_out.at[0], low_ref, up), (face_out.at[1], high_ref, down),
            ]
        )
    ]
    halos[0].start()
    halos[1].start()

    def push_near_rows(k, carry):
        pltpu.make_async_remote_copy(
            near_rows.at[g], near_rows.at[g], rows_send.at[0], rows_recv.at[0],
            device_id=(offset_peer(g, k), s), device_id_type=MESH,
        ).start()
        return carry

    lax.fori_loop(0, GROUPS - 1, push_near_rows, 0)
    total[...] = add_up(recv, [g])
    halos[0].wait_recv()
    halos[1].wait_recv()
    lane = iota((8, 128), 1)
    own_half, turn = lane < 64, lane & 7

    def extended(own, below, above):
        beyond = jnp.where(turn == 7, below, jnp.where(turn == 0, above, 0.0))
        return jnp.where(own_half, own, pltpu.roll(beyond, 64, axis=1))

    share, edges = [
        extended(static[rows, :], low_in[rows, :], high_in[rows, :]) for rows in (slice(0, 8), slice(8, 16))
    ]
    edges = edges.astype(I32)
    sublane = iota((128, 128), 0)

    def locate(node):
        group, span, local = node >> 9, (node >> 6) & 7, node & 63
        return span * 16 + (group >> 1), (group & 1) * 64 + local

    here = iota((1, 128), 1)
    below = (g * SPANS + down) * 64 + here - 64
    above = (g * SPANS + up) * 64 + here - 64
    itself = jnp.where(here < 64, (g * SPANS + s) * 64 + here, jnp.where((here & 7) == 7, below, above))
    for d in range(7):
        line, column = locate(edges[d : d + 1, :] if d < 6 else itself)
        cols = slice(d * 128, (d + 1) * 128)
        picks[:, cols] = jnp.where(sublane == column, 1.0, 0.0).astype(BF16)
        weights[:, cols] = jnp.where(sublane == line, share[d : d + 1, :] if d < 6 else 1.0, 0.0)

    wait_for(near_rows.at[pl.ds(0, GROUPS - 1)], rows_recv.at[0])
    for h in range(16):
        even, odd = near_rows[2 * h], near_rows[2 * h + 1]
        pair = jnp.where(own_half, even, pltpu.roll(odd, 64, axis=1))
        ends = jnp.where(own_half, pltpu.roll(even, 64, axis=1), odd)
        for d in range(6):
            far_rows[s, d * 16 + h : d * 16 + h + 1, :] = pair[d : d + 1, :]
            far_rows[s, 96 + d * 16 + h : 96 + d * 16 + h + 1, :] = ends[d : d + 1, :]

    def push_far_rows(k, carry):
        pltpu.make_async_remote_copy(
            far_rows.at[s], far_rows.at[s], rows_send.at[1], rows_recv.at[1],
            device_id=(g, (s + k) % SPANS), device_id_type=MESH,
        ).start()
        return carry

    lax.fori_loop(1, SPANS, push_far_rows, 0)
    for k in range(0, GROUPS - 1, TOGETHER):
        sources = [offset_peer(g, n) for n in range(k, min(k + TOGETHER, GROUPS - 1))]
        for source in sources:
            wait_for(recv.at[source], recv_sem.at[source])
        total[...] += add_up(recv, sources)

    row = iota((8, 128), 0)
    first = jnp.zeros((8, 128), F32)
    for c in range(3):
        sums = total[2 * c * NP : (2 * c + 1) * NP, :] + total[(2 * c + 1) * NP : (2 * c + 2) * NP, :]
        load = jnp.sum(sums, axis=0, keepdims=True)
        load = load[:, 0:128] + load[:, 128:256]
        load = load + pltpu.roll(load, 64, axis=1)
        value = (force_ref[c : c + 1, :] + 0.25 * load[:, 0:64]) / diagonal
        first = jnp.where(row == c, jnp.concatenate([value, value], axis=1), first)
        total[2 * c * NP : (2 * c + 1) * NP, :] = sums
    def place(state):
        state = jnp.where(own_half, state, 0.0)
        return jnp.where(g % 2 == 1, pltpu.roll(state, 64, axis=1), state)[0:4, :]

    def push_near(r):
        def push(k, carry):
            pltpu.make_async_remote_copy(
                near.at[r, g], near.at[r, g], near_send.at[r], near_recv.at[r],
                device_id=(offset_peer(g, k), s), device_id_type=MESH,
            ).start()
            return carry

        lax.fori_loop(0, GROUPS - 1, push, 0)

    near[0, g] = place(first)
    push_near(0)
    for c in range(3):
        full = jnp.concatenate([total[2 * c * NP : (2 * c + 1) * NP, :], jnp.zeros((128 - NP, 256), F32)], axis=0)
        faces_ref[c] = full.T
    for c in range(3):
        face_out[0, c] = faces_ref[c, pl.ds(7, 32, stride=8), :]
        face_out[1, c] = faces_ref[c, pl.ds(0, 32, stride=8), :]
    halos[2].start()
    halos[3].start()
    wait_for(far_rows.at[pl.ds(0, SPANS - 1)], rows_recv.at[1])
    links = [static[8 + d : 9 + d, :].astype(I32) for d in range(6)]
    joint = [jnp.where(here < 64, links[2 * t], pltpu.roll(links[2 * t + 1], 64, axis=1)) for t in range(3)]
    parts = [static[d : d + 1, :] for d in range(6)]
    shares = [jnp.where(here < 64, parts[2 * t], pltpu.roll(parts[2 * t + 1], 64, axis=1)) for t in range(3)]
    rows_table = jnp.concatenate(split(far_rows[...].reshape(SPANS * 192, 128)), axis=1)
    for t in range(3):
        line, column = locate(joint[t])
        pick = jnp.where(sublane == column, 1.0, 0.0).astype(BF16)
        found = jnp.dot(rows_table, jnp.concatenate([pick, pick], axis=0), preferred_element_type=F32)
        found = found.reshape(SPANS, 12, 16, 128)
        mask = jnp.where(sublane == line, 1.0, 0.0).reshape(SPANS, 16, 128)
        for d in range(6):
            share2 = jnp.sum((found[:, d] * mask).reshape(128, 128), axis=0, keepdims=True)
            link2 = jnp.sum((found[:, 6 + d] * mask).reshape(128, 128), axis=0, keepdims=True)
            line2, column2 = locate(link2.astype(I32))
            cols = slice((t * 6 + d) * 128, (t * 6 + d + 1) * 128)
            picks2[:, cols] = jnp.where(sublane == column2, 1.0, 0.0).astype(BF16)
            weights2[:, cols] = jnp.where(sublane == line2, share2 * shares[t], 0.0)

    def combine(table, pick, weight):
        table = jnp.concatenate(split(table), axis=1)
        out = jnp.zeros((8, 128), F32)
        found = jnp.dot(table, jnp.concatenate([pick, pick], axis=0), preferred_element_type=F32)
        width = pick.shape[1]
        found = found.reshape(SPANS, 3, 16, width)
        weighted = weight.reshape(SPANS, 16, width)
        for c in range(3):
            sums = jnp.sum((found[:, c] * weighted).reshape(SPANS * 16, width), axis=0, keepdims=True)
            parts = [sums[:, d * 128 : (d + 1) * 128] for d in range(width // 128)]
            out = jnp.where(row == c, functools.reduce(jnp.add, parts), out)
        return out

    for r in range(ROUNDS):
        wait_for(near.at[r, pl.ds(0, GROUPS - 1)], near_recv.at[r])
        for h in range(16):
            pair = near[r, 2 * h] + near[r, 2 * h + 1]
            for c in range(3):
                far[r, s, c * 16 + h : c * 16 + h + 1, :] = pair[c : c + 1, :]

        def push(k, carry):
            peer = (s + k) % SPANS
            pltpu.make_async_remote_copy(
                far.at[r, s], far.at[r, s], far_send.at[r], far_recv.at[r],
                device_id=(g, peer), device_id_type=MESH,
            ).start()
            return carry

        lax.fori_loop(1, SPANS, push, 0)
        wait_for(far.at[r, pl.ds(0, SPANS - 1)], far_recv.at[r])
        table = far[r].reshape(SPANS * 48, 128)
        if r == 0:
            sums = combine(table, picks2[...], weights2[...])
            near[1, g] = place(first + sums + pltpu.roll(sums, 64, axis=1))
            push_near(1)
        else:
            state = combine(table, picks[...], weights[...])
    skel_ref[...] = state
    halos[2].wait_recv()
    halos[3].wait_recv()
    wait_for(send.at[pl.ds(0, GROUPS - 1)], send_sem)
    for halo in halos:
        halo.wait_send()
    wait_for(near_rows.at[pl.ds(0, GROUPS - 1)], rows_send.at[0])
    wait_for(far_rows.at[pl.ds(0, SPANS - 1)], rows_send.at[1])
    for r in range(ROUNDS):
        wait_for(near.at[r, pl.ds(0, GROUPS - 1)], near_send.at[r])
        wait_for(far.at[r, pl.ds(0, SPANS - 1)], far_send.at[r])


def front(disp, weight, owner, row, force, coupling, stiff, edges):
    dma = pltpu.SemaphoreType.DMA
    local = [pltpu.VMEM(x.shape, x.dtype) for x in (disp, weight, owner, row, force, coupling, stiff, edges)]
    return pl.pallas_call(
        front_body,
        name="front",
        out_shape=(
            jax.ShapeDtypeStruct((3, 256, 128), F32),
            jax.ShapeDtypeStruct((8, 128), F32),
            jax.ShapeDtypeStruct((3, 32, 128), F32),
            jax.ShapeDtypeStruct((3, 32, 128), F32),
        ),
        in_specs=[pl.BlockSpec(memory_space=pltpu.HBM)] * 8,
        out_specs=(VMEM_SPEC,) * 4,
        scratch_shapes=[
            *local,
            pltpu.VMEM((512, NODES), BF16), pltpu.VMEM((256, NODES), BF16),
            pltpu.VMEM((GROUPS, 8, 256), F32), pltpu.VMEM((GROUPS, 8, 256), F32),
            pltpu.VMEM((6 * NP, 256), F32),
            pltpu.VMEM((16, 128), F32), pltpu.VMEM((16, 128), F32), pltpu.VMEM((16, 128), F32),
            pltpu.VMEM((2, 3, 32, 128), F32),
            pltpu.VMEM((ROUNDS, GROUPS, 4, 128), F32),
            pltpu.VMEM((ROUNDS, SPANS, 48, 128), F32),
            pltpu.VMEM((128, 896), BF16), pltpu.VMEM((128, 896), F32),
            pltpu.VMEM((GROUPS, 8, 128), F32), pltpu.VMEM((SPANS, 192, 128), F32),
            pltpu.VMEM((128, 2304), BF16), pltpu.VMEM((128, 2304), F32),
            dma((8,)), dma, dma((GROUPS,)),
            dma((ROUNDS,)), dma((ROUNDS,)), dma((ROUNDS,)), dma((ROUNDS,)), dma((4,)), dma((4,)),
            dma((2,)), dma((2,)),
        ],
        compiler_params=pltpu.CompilerParams(
            collective_id=0, has_side_effects=True, vmem_limit_bytes=63 << 20
        ),
    )(disp, weight, owner, row, force, coupling, stiff, edges)


HALF = NP * NP // 2
CHUNK = 640
CHUNKS = NP * NP // CHUNK


def blend_table():
    f = np.arange(NP * NP)
    i, j = f % NP, f // NP
    n = NP - 1

    def bubble(i, j):
        s, t = i / n, j / n
        return 16.0 * s * (1 - s) * t * (1 - t)

    ip, im = np.minimum(i + 1, n), np.maximum(i - 1, 0)
    jp, jm = np.minimum(j + 1, n), np.maximum(j - 1, 0)
    hit = (j[None] % 40 == np.arange(40)[:, None]).astype(np.float64)
    rows = [hit, hit * i, hit * (ip - im)]
    for bump in (
        bubble(i, j), 0.5 * (bubble(ip, j) - bubble(im, j)), 0.5 * (bubble(i, jp) - bubble(i, jm))
    ):
        high = bump.astype(BF16).astype(np.float64)
        rows += [high[None], (bump - high)[None]]
    rows.append(np.zeros((2, NP * NP)))
    return np.concatenate(rows).astype(BF16)


def column_of(values):
    return jnp.concatenate([jnp.full((8, 128), value, F32) for value in values], axis=0)


def prepare(faces_ref, low_ref, high_ref, spacing_ref, lhs_ref, fns_ref):
    span = lax.axis_index("span")
    has_low = jnp.where(span > 0, 1.0, 0.0).astype(F32)
    has_high = jnp.where(span < SPANS - 1, 1.0, 0.0).astype(F32)
    lane = iota((LAYERS, 128), 1)
    turn = iota((LAYERS, 128), 0) & 7
    frac = lane.astype(F32) * (1.0 / (NP - 1))

    def along_span(x, c, seg):
        rows = [slice(seg * 8 + q, seg * 8 + q + 1) for q in range(8)]
        before = jnp.concatenate([jnp.broadcast_to(low_ref[c, r, :], (8, 128)) for r in rows], axis=0)
        after = jnp.concatenate([jnp.broadcast_to(high_ref[c, r, :], (8, 128)) for r in rows], axis=0)
        nxt = jnp.where(turn == 7, after * has_high, pltpu.roll(x, LAYERS - 1, axis=0))
        prv = jnp.where(turn == 0, before * has_low, pltpu.roll(x, 1, axis=0))
        return 0.5 * (nxt - prv)

    def along_lane(x):
        nxt = jnp.where(lane == NP - 1, x, pltpu.roll(x, 127, axis=1))
        prv = jnp.where(lane == 0, x, pltpu.roll(x, 1, axis=1))
        return 0.5 * (nxt - prv)

    def inner(x):
        return x - (1.0 - frac) * x[:, 0:1] - frac * x[:, NP - 1 : NP]

    for c in range(3):
        now = [faces_ref[c, seg * LAYERS : (seg + 1) * LAYERS, :] for seg in range(4)]
        diff = [along_span(x, c, seg) for seg, x in enumerate(now)]
        values = []
        for bottom, top, left, right in (now, diff):
            base = inner(bottom)
            values.append((base, inner(top) - base, left, (right - left) * (1.0 / (NP - 1))))
        (b, d, left, m), (b_s, d_s, left_s, m_s) = values
        b_i, left_j = along_lane(b), along_lane(left)
        if c == 0:
            b_i = b_i + column_of([spacing_ref[c, q] for q in range(8)])
        elif c == 1:
            left_j = left_j + column_of([spacing_ref[c, q] for q in range(8)])
        else:
            b_s = b_s + column_of([spacing_ref[c, q] for q in range(8)])
        for n, fn in enumerate((b, d, b_i, along_lane(d), b_s, d_s)):
            for phase in range(5):
                at = lane[0:8] + (phase * 128) % NP
                at = jnp.where(at >= NP, at - NP, at)
                at = jnp.where(at >= NP, at - NP, at)
                for q in range(8):
                    rows = slice(q * 8, q * 8 + 8)
                    fns_ref[phase, n, c, rows, :] = jnp.take_along_axis(fn[rows], at, axis=1)
        for half in range(2):
            shift = (128 - 40 * half) % 128
            fields = [None] * 4
            for n, (x, y) in ((0, (left, m)), (2, (left_j, along_lane(m))), (3, (left_s, m_s))):
                x = pltpu.roll(x, shift, axis=1) if half else x
                y = y if half else pltpu.roll(y, 40, axis=1)
                fields[n] = jnp.where(lane < 40, x, jnp.where(lane < 80, y, 0.0))
            x = pltpu.roll(0.5 * m, 40 if half else 80, axis=1)
            fields[1] = jnp.where((lane >= 80) & (lane < 120), x, 0.0)
            for n, field in enumerate(fields):
                high, low = split(field)
                rows = slice((n * 3 + c) * LAYERS, (n * 3 + c + 1) * LAYERS)
                lhs_ref[half, rows, 0:128] = high
                lhs_ref[half, rows, 128:256] = low


def place_bumps(skel_ref, lhs_ref):
    span = lax.axis_index("span")
    has_low = jnp.where(span > 0, 1.0, 0.0).astype(F32)
    has_high = jnp.where(span < SPANS - 1, 1.0, 0.0).astype(F32)
    lane, row = iota((LAYERS, 128), 1), iota((LAYERS, 128), 0)
    turn = row & 7
    for c in range(3):
        skel = jnp.broadcast_to(skel_ref[c : c + 1, :], (LAYERS, 128))

        def column(where):
            return jnp.sum(jnp.where(where, skel, 0.0), axis=1, keepdims=True)

        value = column(lane == row)
        nxt = column(lane == jnp.where(turn == 7, 64 + row - 7, row + 1))
        prv = column(lane == jnp.where(turn == 0, 64 + row + 7, row - 1))
        nxt = jnp.where(turn[:, 0:1] == 7, nxt * has_high, nxt)
        prv = jnp.where(turn[:, 0:1] == 0, prv * has_low, prv)
        diff = 0.5 * (nxt - prv)
        for n, (x, first) in enumerate(((value, 120), (value, 122), (value, 124), (diff, 120))):
            rows = slice((n * 3 + c) * LAYERS, (n * 3 + c + 1) * LAYERS)
            mine = (lane == first) | (lane == first + 1)
            for part, cols in zip(split(jnp.where(mine, x, 0.0)), (slice(0, 128), slice(128, 256))):
                for half in range(2):
                    lhs_ref[half, rows, cols] = lhs_ref[half, rows, cols] + part


def blend_body(
    spacing_ref, faces_hbm, low_hbm, high_hbm, skel_hbm, table_hbm, disp_hbm, jac_hbm,
    faces_ref, low_ref, high_ref, skel_ref, table_ref, lhs_ref, fns_ref, even, odd, disp_ref, jac_ref,
    load_sem, store_sem,
):
    loads = [
        pltpu.make_async_copy(src, dst, load_sem.at[n])
        for n, (src, dst) in enumerate(
            [
                (faces_hbm, faces_ref), (low_hbm, low_ref), (high_hbm, high_ref), (skel_hbm, skel_ref),
                (table_hbm, table_ref),
            ]
        )
    ]
    for load in loads:
        load.start()
    for load in loads[:4]:
        load.wait()
    prepare(faces_ref, low_ref, high_ref, spacing_ref, lhs_ref, fns_ref)
    place_bumps(skel_ref, lhs_ref)
    loads[4].wait()

    def cols_of(n):
        return pl.ds(pl.multiple_of(n * CHUNK, 128), CHUNK)

    def multiply(n, out):
        table = table_ref[:, cols_of(n)]
        out[...] = jnp.dot(
            lhs_ref[n // (CHUNKS // 2)], jnp.concatenate([table, table], axis=0), preferred_element_type=F32
        )

    def finish(n, found):
        place = iota((8, 128), 1)
        for phase in range(5):
            cols = slice(phase * 128, (phase + 1) * 128)
            far = place + phase * 128
            j = n * (CHUNK // NP) + sum(jnp.where(far >= NP * k, 1, 0) for k in range(1, CHUNK // NP))
            t = j.astype(F32) * (1.0 / (NP - 1))
            t_j = jnp.where((j == 0) | (j == NP - 1), 0.5 / (NP - 1), 1.0 / (NP - 1))
            out_cols = pl.ds(pl.multiple_of(n * CHUNK + phase * 128, 128), 128)
            for q in range(8):
                matrix = []
                for c in range(3):
                    b, d, b_i, d_i, b_s, d_s = [
                        fns_ref[phase, k, c, q * 8 : q * 8 + 8, :] for k in range(6)
                    ]
                    x, x_i, x_j, x_s = [
                        found[(k * 3 + c) * LAYERS + q * 8 : (k * 3 + c) * LAYERS + q * 8 + 8, cols]
                        for k in range(4)
                    ]
                    disp_ref[c, q, :, out_cols] = x + b + t * d
                    matrix.append([x_i + b_i + t * d_i, x_j + t_j * d, x_s + b_s + t * d_s])
                one = matrix[1][1] * matrix[2][2] - matrix[1][2] * matrix[2][1]
                two = matrix[1][0] * matrix[2][2] - matrix[1][2] * matrix[2][0]
                three = matrix[1][0] * matrix[2][1] - matrix[1][1] * matrix[2][0]
                jac_ref[q, :, out_cols] = matrix[0][0] * one - matrix[0][1] * two + matrix[0][2] * three

    def stores(n):
        cols = cols_of(n)
        return (
            pltpu.make_async_copy(disp_ref.at[:, :, :, cols], disp_hbm.at[:, :, :, cols], store_sem.at[0, n]),
            pltpu.make_async_copy(jac_ref.at[:, :, cols], jac_hbm.at[:, :, cols], store_sem.at[1, n]),
        )

    multiply(0, even)

    def step(k, carry):
        n = 2 * k
        multiply(n + 1, odd)
        finish(n, even)
        for store in stores(n):
            store.start()
        multiply(jnp.minimum(n + 2, CHUNKS - 1), even)
        finish(n + 1, odd)
        for store in stores(n + 1):
            store.start()
        return carry

    lax.fori_loop(0, CHUNKS // 2, step, 0)

    def drain(n, carry):
        for store in stores(n):
            store.wait()
        return carry

    lax.fori_loop(0, CHUNKS, drain, 0)


def blend(spacing, faces, low, high, skel):
    any_spec = pl.BlockSpec(memory_space=pl.ANY)
    table = blend_table()
    return pl.pallas_call(
        blend_body,
        name="blend",
        out_shape=(
            jax.ShapeDtypeStruct((3, 8, 8, NP * NP), F32),
            jax.ShapeDtypeStruct((8, 8, NP * NP), F32),
        ),
        in_specs=[pl.BlockSpec(memory_space=pltpu.SMEM)] + [any_spec] * 5,
        out_specs=(any_spec, any_spec),
        scratch_shapes=[
            pltpu.VMEM(faces.shape, F32), pltpu.VMEM(low.shape, F32), pltpu.VMEM(high.shape, F32),
            pltpu.VMEM(skel.shape, F32), pltpu.VMEM(table.shape, BF16),
            pltpu.VMEM((2, 12 * LAYERS, 256), BF16), pltpu.VMEM((5, 6, 3, LAYERS, 128), F32),
            pltpu.VMEM((12 * LAYERS, CHUNK), F32), pltpu.VMEM((12 * LAYERS, CHUNK), F32),
            pltpu.VMEM((3, 8, 8, NP * NP), F32), pltpu.VMEM((8, 8, NP * NP), F32),
            pltpu.SemaphoreType.DMA((5,)), pltpu.SemaphoreType.DMA((2, CHUNKS)),
        ],
        compiler_params=pltpu.CompilerParams(vmem_limit_bytes=63 << 20),
    )(spacing, faces, low, high, skel, jnp.asarray(table))


def on_device(disp, weight, owner, row, force, coupling, stiff, edges, spacing):
    faces, skel, low, high = front(
        disp, weight.T, owner.T, row.T, force, coupling, stiff.reshape(1, -1), edges
    )
    return blend(spacing, faces, low, high, skel)


def solution(mesh):
    return jax.shard_map(
        on_device,
        mesh=mesh,
        in_specs=(
            P(None, ("group", "span")),
            P(("group", "span"), None),
            P(("group", "span"), None),
            P(("group", "span"), None),
            P(None, ("group", "span")),
            P(None, ("group", "span")),
            P(("group", "span")),
            P(None, ("group", "span")),
            P(None, "group"),
        ),
        out_specs=(P(None, "group", "span", None), P("group", "span", None)),
        check_vma=False,
    )
```

```python
import functools

import jax
import jax.numpy as jnp
import numpy as np
from jax import lax
from jax.experimental import pallas as pl
from jax.experimental.pallas import tpu as pltpu
from jax.sharding import PartitionSpec as P

F32, BF16, I32 = jnp.float32, jnp.bfloat16, jnp.int32
NP = 80
LAYERS = 64
GROUPS, SPANS = 32, 8
NODES = 2048
MESH = pl.DeviceIdType.MESH
NT = (((1,), (1,)), ((), ()))
VMEM_SPEC = pl.BlockSpec(memory_space=pltpu.VMEM)


def iota(shape, dim):
    return lax.broadcasted_iota(I32, shape, dim)


def split(value):
    high = value.astype(BF16)
    return high, (value - high.astype(F32)).astype(BF16)


CHUNK_J = 16
CHUNK = CHUNK_J * NP
CHUNKS = NP // CHUNK_J


def blend_table():
    f = np.arange(NP * NP)
    i, j = f % NP, f // NP
    n = NP - 1

    def bubble(i, j):
        s, t = i / n, j / n
        return 16.0 * s * (1 - s) * t * (1 - t)

    ip, im = np.minimum(i + 1, n), np.maximum(i - 1, 0)
    jp, jm = np.minimum(j + 1, n), np.maximum(j - 1, 0)
    hit = (j[None] % CHUNK_J == np.arange(CHUNK_J)[:, None]).astype(np.float64)
    rows = [hit, hit * i, hit * (ip - im)]
    for bump in (
        bubble(i, j), 0.5 * (bubble(ip, j) - bubble(im, j)), 0.5 * (bubble(i, jp) - bubble(i, jm))
    ):
        high = bump.astype(BF16).astype(np.float64)
        rows += [high[None], (bump - high)[None]]
    rows.append(np.zeros((10, NP * NP)))
    return np.concatenate(rows).astype(BF16)


def column_of(values):
    return jnp.concatenate([jnp.full((8, 128), value, F32) for value in values], axis=0)


def two_parts(x, lane):
    x = x + pltpu.roll(x, 64, axis=1)
    high = x.astype(BF16).astype(F32)
    return jnp.where(lane < 64, high, x - high).astype(BF16)


def prepare(faces_ref, low_ref, high_ref, spacing_ref, lhs_ref, fns_ref):
    span = lax.axis_index("span")
    has_low = jnp.where(span > 0, 1.0, 0.0).astype(F32)
    has_high = jnp.where(span < SPANS - 1, 1.0, 0.0).astype(F32)
    lane = iota((LAYERS, 128), 1)
    turn = iota((LAYERS, 128), 0) & 7
    frac = lane.astype(F32) * (1.0 / (NP - 1))

    def along_span(x, c, seg):
        rows = [slice(seg * 8 + q, seg * 8 + q + 1) for q in range(8)]
        before = jnp.concatenate([jnp.broadcast_to(low_ref[c, r, :], (8, 128)) for r in rows], axis=0)
        after = jnp.concatenate([jnp.broadcast_to(high_ref[c, r, :], (8, 128)) for r in rows], axis=0)
        nxt = jnp.where(turn == 7, after * has_high, pltpu.roll(x, LAYERS - 1, axis=0))
        prv = jnp.where(turn == 0, before * has_low, pltpu.roll(x, 1, axis=0))
        return 0.5 * (nxt - prv)

    def along_lane(x):
        nxt = jnp.where(lane == NP - 1, x, pltpu.roll(x, 127, axis=1))
        prv = jnp.where(lane == 0, x, pltpu.roll(x, 1, axis=1))
        return 0.5 * (nxt - prv)

    def inner(x):
        return x - (1.0 - frac) * x[:, 0:1] - frac * x[:, NP - 1 : NP]

    for c in range(3):
        now = [faces_ref[c, seg * LAYERS : (seg + 1) * LAYERS, :] for seg in range(4)]
        diff = [along_span(x, c, seg) for seg, x in enumerate(now)]
        values = []
        for bottom, top, left, right in (now, diff):
            base = inner(bottom)
            values.append((base, inner(top) - base, left, (right - left) * (1.0 / (NP - 1))))
        (b, d, left, m), (b_s, d_s, left_s, m_s) = values
        b_i, left_j = along_lane(b), along_lane(left)
        if c == 0:
            b_i = b_i + column_of([spacing_ref[c, q] for q in range(8)])
        elif c == 1:
            left_j = left_j + column_of([spacing_ref[c, q] for q in range(8)])
        else:
            b_s = b_s + column_of([spacing_ref[c, q] for q in range(8)])
        for n, fn in enumerate((b, d, b_i, along_lane(d), b_s, d_s)):
            fns_ref[n, c] = fn
        m_j = along_lane(m)
        for chunk in range(CHUNKS):

            def at(x, first):
                shift = (first - chunk * CHUNK_J) % 128
                return pltpu.roll(x, shift, axis=1) if shift else x

            fields = [
                jnp.where(lane < 16, at(x, 0), jnp.where(lane < 32, at(y, 16), 0.0))
                for x, y in ((left, m), (left_j, m_j), (left_s, m_s))
            ]
            fields.insert(1, jnp.where((lane >= 32) & (lane < 48), at(0.5 * m, 32), 0.0))
            for n, field in enumerate(fields):
                lhs_ref[chunk, (n * 3 + c) * LAYERS : (n * 3 + c + 1) * LAYERS, :] = two_parts(field, lane)


def wait_for(ref, sem):
    pltpu.make_async_copy(ref, ref, sem).wait()


def offset_peer(g, k):
    n, m = k // 4, k % 4
    dz = 4 + ((n + 1) // 2) * (1 - 2 * (n % 2))
    dx = 2 + ((m + 1) // 2) * (1 - 2 * (m % 2))
    return ((g // 8 + dx) % 4) * 8 + (g % 8 + dz) % 8


def pack(disp_ref, weight_ref, owner_ref, row_ref, out_ref, lhs, rhs):
    group_rows = iota((GROUPS, NODES), 0)
    present = jnp.zeros((GROUPS, NODES), F32)
    for t in range(4):
        present += jnp.where(owner_ref[t : t + 1, :] == group_rows, 1.0, 0.0)
    present = present.astype(BF16)
    before = jnp.where(iota((256, 256), 0) < iota((256, 256), 1), 1.0, 0.0).astype(BF16)
    every = jnp.ones((256, 256), BF16)
    base = jnp.zeros((GROUPS, 256), F32)
    ranks = []
    for k in range(NODES // 256):
        piece = present[:, k * 256 : (k + 1) * 256]
        ranks.append(jnp.dot(piece, before, preferred_element_type=F32) + base)
        base += jnp.dot(piece, every, preferred_element_type=F32)
    rank = jnp.concatenate(ranks, axis=1)
    word = iota((8, NODES), 0) & 3
    total = jnp.zeros((512, 256), F32)
    for t in range(4):
        owner = owner_ref[t : t + 1, :]
        slot = jnp.sum(jnp.where(owner == group_rows, rank, 0.0), axis=0, keepdims=True).astype(I32)
        half = slot >> 8
        column = slot & 255
        bucket = owner * 2 + half
        row = row_ref[t : t + 1, :]
        layer = ((row >> 6) * 205) >> 10
        edge = row - layer * (4 * NP)
        seg = ((edge >> 4) * 205) >> 10
        along = (edge - seg * NP) << 8
        line = seg * LAYERS + layer
        weight = weight_ref[t : t + 1, :]
        value = jnp.where(
            word == 0, disp_ref[0:1, :], jnp.where(word == 1, disp_ref[1:2, :], disp_ref[2:3, :])
        ) * weight
        high = jnp.where(word == 3, along.astype(F32), value).astype(BF16)
        low = jnp.where(word == 3, line.astype(F32), value - high.astype(F32)).astype(BF16)
        high = jnp.concatenate([high] * 32, axis=0)
        low = jnp.concatenate([low] * 32, axis=0)
        hit = (iota((256, NODES), 0) >> 2) == bucket
        zero = jnp.zeros((), BF16)
        lhs[0:256, :] = jnp.where(hit, high, zero)
        lhs[256:512, :] = jnp.where(hit, low, zero)
        rhs[...] = jnp.where(iota((256, NODES), 0) == column, 1.0, 0.0).astype(BF16)
        total += lax.dot_general(lhs[...], rhs[...], NT, preferred_element_type=F32)
    out_ref[...] = (total[0:256] + total[256:512]).reshape(GROUPS, 8, 256)


def add_up(recv_ref, sources):
    lines = iota((256, 256), 0)
    places = iota((NP, 256), 0)
    zero = jnp.zeros((), BF16)
    lhs, rhs = [], []
    for source in sources:
        for h in range(2):
            code = recv_ref[source, 4 * h + 3 : 4 * h + 4, :].astype(I32)
            hit = places == (code >> 8)
            parts = []
            for c in range(3):
                for part in split(recv_ref[source, 4 * h + c : 4 * h + c + 1, :]):
                    parts.append(jnp.where(hit, jnp.broadcast_to(part, (NP, 256)), zero))
            lhs.append(jnp.concatenate(parts, axis=0))
            rhs.append(jnp.where(lines == (code & 255), 1.0, 0.0).astype(BF16))
    return lax.dot_general(
        jnp.concatenate(lhs, axis=1), jnp.concatenate(rhs, axis=1), NT, preferred_element_type=F32
    )


ROUNDS = 2
TOGETHER = 4


def front_body(
    disp_hbm, weight_hbm, owner_hbm, row_hbm, force_hbm, coupling_hbm, stiff_hbm, edges_hbm,
    spacing_hbm, lhs_hbm, fns_hbm, skel_ref,
    disp_ref, weight_ref, owner_ref, row_ref, force_ref, coupling_ref, stiff_ref, edges_ref,
    spacing_ref, faces_ref, low_ref, high_ref, lhs_ref, fns_ref, lhs, rhs, send, recv, total,
    static, low_in, high_in, face_out, near, far, picks, weights, near_rows, far_rows, picks2, weights2,
    load_sem, send_sem, recv_sem, near_send, near_recv, far_send, far_recv, halo_send, halo_recv,
    rows_send, rows_recv, result_sem,
):
    g, s = lax.axis_index("group"), lax.axis_index("span")
    up, down = (s + 1) % SPANS, (s + SPANS - 1) % SPANS
    loads = [
        pltpu.make_async_copy(src, dst, load_sem.at[n])
        for n, (src, dst) in enumerate(
            [
                (owner_hbm, owner_ref), (row_hbm, row_ref), (disp_hbm, disp_ref), (weight_hbm, weight_ref),
                (coupling_hbm, coupling_ref), (stiff_hbm, stiff_ref), (edges_hbm, edges_ref), (force_hbm, force_ref),
                (spacing_hbm, spacing_ref),
            ]
        )
    ]
    for load in loads:
        load.start()
    barrier = pltpu.get_barrier_semaphore()

    def greet_group(k, carry):
        pl.semaphore_signal(barrier, inc=1, device_id=(offset_peer(g, k), s), device_id_type=MESH)
        return carry

    def greet_span(k, carry):
        pl.semaphore_signal(barrier, inc=1, device_id=(g, (s + k) % SPANS), device_id_type=MESH)
        return carry

    lax.fori_loop(0, GROUPS - 1, greet_group, 0)
    lax.fori_loop(1, SPANS, greet_span, 0)
    for load in loads:
        load.wait()
    diagonal = stiff_ref[...] + jnp.sum(coupling_ref[...], axis=0, keepdims=True)
    share_rows, edge_rows = coupling_ref[...] / diagonal, edges_ref[...].astype(F32)
    blank = jnp.zeros((6, 64), F32)
    static[0:6, :] = jnp.concatenate([share_rows, blank], axis=1)
    static[8:14, :] = jnp.concatenate([edge_rows, blank], axis=1)
    near_rows[g] = jnp.concatenate(
        [jnp.concatenate([share_rows, edge_rows], axis=1), jnp.zeros((2, 128), F32)], axis=0
    )
    pl.semaphore_wait(barrier, GROUPS - 1 + SPANS - 1)

    def push_near_rows(k, carry):
        pltpu.make_async_remote_copy(
            near_rows.at[g], near_rows.at[g], rows_send.at[0], rows_recv.at[0],
            device_id=(offset_peer(g, k), s), device_id_type=MESH,
        ).start()
        return carry

    lax.fori_loop(0, GROUPS - 1, push_near_rows, 0)
    pack(disp_ref, weight_ref, owner_ref, row_ref, send, lhs, rhs)

    def push_send(k, carry):
        peer = offset_peer(g, k)
        pltpu.make_async_remote_copy(
            send.at[peer], recv.at[g], send_sem, recv_sem.at[g], device_id=(peer, s), device_id_type=MESH
        ).start()
        return carry

    lax.fori_loop(0, GROUPS - 1, push_send, 0)
    own = pltpu.make_async_copy(send.at[g], recv.at[g], recv_sem.at[g])
    own.start()
    halos = [
        pltpu.make_async_remote_copy(
            src, dst, halo_send.at[n], halo_recv.at[n], device_id=(g, to), device_id_type=MESH
        )
        for n, (src, dst, to) in enumerate(
            [
                (static, low_in, up), (static, high_in, down),
                (face_out.at[0], low_ref, up), (face_out.at[1], high_ref, down),
            ]
        )
    ]
    halos[0].start()
    halos[1].start()
    total[...] = jnp.zeros_like(total)
    halos[0].wait_recv()
    halos[1].wait_recv()
    lane = iota((8, 128), 1)
    own_half, turn = lane < 64, lane & 7

    def extended(own, below, above):
        beyond = jnp.where(turn == 7, below, jnp.where(turn == 0, above, 0.0))
        return jnp.where(own_half, own, pltpu.roll(beyond, 64, axis=1))

    share, edges = [
        extended(static[rows, :], low_in[rows, :], high_in[rows, :]) for rows in (slice(0, 8), slice(8, 16))
    ]
    edges = edges.astype(I32)
    sublane = iota((128, 128), 0)

    def locate(node):
        group, span, local = node >> 9, (node >> 6) & 7, node & 63
        return span * 16 + (group >> 1), (group & 1) * 64 + local

    here = iota((1, 128), 1)
    below = (g * SPANS + down) * 64 + here - 64
    above = (g * SPANS + up) * 64 + here - 64
    itself = jnp.where(here < 64, (g * SPANS + s) * 64 + here, jnp.where((here & 7) == 7, below, above))
    for d in range(7):
        line, column = locate(edges[d : d + 1, :] if d < 6 else itself)
        cols = slice(d * 128, (d + 1) * 128)
        picks[:, cols] = jnp.where(sublane == column, 1.0, 0.0).astype(BF16)
        weights[:, cols] = jnp.where(sublane == line, share[d : d + 1, :] if d < 6 else 1.0, 0.0)

    wait_for(near_rows.at[pl.ds(0, GROUPS - 1)], rows_recv.at[0])
    for h in range(16):
        even, odd = near_rows[2 * h], near_rows[2 * h + 1]
        pair = jnp.where(own_half, even, pltpu.roll(odd, 64, axis=1))
        ends = jnp.where(own_half, pltpu.roll(even, 64, axis=1), odd)
        for d in range(6):
            far_rows[s, d * 16 + h : d * 16 + h + 1, :] = pair[d : d + 1, :]
            far_rows[s, 96 + d * 16 + h : 96 + d * 16 + h + 1, :] = ends[d : d + 1, :]

    def push_far_rows(k, carry):
        pltpu.make_async_remote_copy(
            far_rows.at[s], far_rows.at[s], rows_send.at[1], rows_recv.at[1],
            device_id=(g, (s + k) % SPANS), device_id_type=MESH,
        ).start()
        return carry

    lax.fori_loop(1, SPANS, push_far_rows, 0)

    def collect(m, carry):
        sources = [offset_peer(g, m * TOGETHER + u) for u in range(TOGETHER)]
        for source in sources:
            wait_for(recv.at[source], recv_sem.at[source])
        total[...] += add_up(recv, sources)
        return carry

    lax.fori_loop(0, GROUPS // TOGETHER, collect, 0)
    row = iota((8, 128), 0)
    first = jnp.zeros((8, 128), F32)
    for c in range(3):
        sums = total[2 * c * NP : (2 * c + 1) * NP, :] + total[(2 * c + 1) * NP : (2 * c + 2) * NP, :]
        load = jnp.sum(sums, axis=0, keepdims=True)
        load = load[:, 0:128] + load[:, 128:256]
        load = load + pltpu.roll(load, 64, axis=1)
        value = (force_ref[c : c + 1, :] + 0.25 * load[:, 0:64]) / diagonal
        first = jnp.where(row == c, jnp.concatenate([value, value], axis=1), first)
        total[2 * c * NP : (2 * c + 1) * NP, :] = sums
    def place(state):
        state = jnp.where(own_half, state, 0.0)
        return jnp.where(g % 2 == 1, pltpu.roll(state, 64, axis=1), state)[0:4, :]

    def push_near(r):
        def push(k, carry):
            pltpu.make_async_remote_copy(
                near.at[r, g], near.at[r, g], near_send.at[r], near_recv.at[r],
                device_id=(offset_peer(g, k), s), device_id_type=MESH,
            ).start()
            return carry

        lax.fori_loop(0, GROUPS - 1, push, 0)

    near[0, g] = place(first)
    push_near(0)
    for c in range(3):
        full = jnp.concatenate([total[2 * c * NP : (2 * c + 1) * NP, :], jnp.zeros((128 - NP, 256), F32)], axis=0)
        faces_ref[c] = full.T
    for c in range(3):
        face_out[0, c] = faces_ref[c, pl.ds(7, 32, stride=8), :]
        face_out[1, c] = faces_ref[c, pl.ds(0, 32, stride=8), :]
    halos[2].start()
    halos[3].start()
    wait_for(far_rows.at[pl.ds(0, SPANS - 1)], rows_recv.at[1])
    links = [static[8 + d : 9 + d, :].astype(I32) for d in range(6)]
    joint = [jnp.where(here < 64, links[2 * t], pltpu.roll(links[2 * t + 1], 64, axis=1)) for t in range(3)]
    parts = [static[d : d + 1, :] for d in range(6)]
    shares = [jnp.where(here < 64, parts[2 * t], pltpu.roll(parts[2 * t + 1], 64, axis=1)) for t in range(3)]
    rows_table = jnp.concatenate(split(far_rows[...].reshape(SPANS * 192, 128)), axis=1)
    for t in range(3):
        line, column = locate(joint[t])
        pick = jnp.where(sublane == column, 1.0, 0.0).astype(BF16)
        found = jnp.dot(rows_table, jnp.concatenate([pick, pick], axis=0), preferred_element_type=F32)
        found = found.reshape(SPANS, 12, 16, 128)
        mask = jnp.where(sublane == line, 1.0, 0.0).reshape(SPANS, 16, 128)
        for d in range(6):
            share2 = jnp.sum((found[:, d] * mask).reshape(128, 128), axis=0, keepdims=True)
            link2 = jnp.sum((found[:, 6 + d] * mask).reshape(128, 128), axis=0, keepdims=True)
            line2, column2 = locate(link2.astype(I32))
            cols = slice((t * 6 + d) * 128, (t * 6 + d + 1) * 128)
            picks2[:, cols] = jnp.where(sublane == column2, 1.0, 0.0).astype(BF16)
            weights2[:, cols] = jnp.where(sublane == line2, share2 * shares[t], 0.0)

    def combine(table, pick, weight):
        table = jnp.concatenate(split(table), axis=1)
        out = jnp.zeros((8, 128), F32)
        found = jnp.dot(table, jnp.concatenate([pick, pick], axis=0), preferred_element_type=F32)
        width = pick.shape[1]
        found = found.reshape(SPANS, 3, 16, width)
        weighted = weight.reshape(SPANS, 16, width)
        for c in range(3):
            sums = jnp.sum((found[:, c] * weighted).reshape(SPANS * 16, width), axis=0, keepdims=True)
            parts = [sums[:, d * 128 : (d + 1) * 128] for d in range(width // 128)]
            out = jnp.where(row == c, functools.reduce(jnp.add, parts), out)
        return out

    results = [
        pltpu.make_async_copy(lhs_ref, lhs_hbm, result_sem.at[0]),
        pltpu.make_async_copy(fns_ref, fns_hbm, result_sem.at[1]),
    ]
    for r in range(ROUNDS):
        wait_for(near.at[r, pl.ds(0, GROUPS - 1)], near_recv.at[r])
        for h in range(16):
            pair = near[r, 2 * h] + near[r, 2 * h + 1]
            for c in range(3):
                far[r, s, c * 16 + h : c * 16 + h + 1, :] = pair[c : c + 1, :]

        def push(k, carry):
            peer = (s + k) % SPANS
            pltpu.make_async_remote_copy(
                far.at[r, s], far.at[r, s], far_send.at[r], far_recv.at[r],
                device_id=(g, peer), device_id_type=MESH,
            ).start()
            return carry

        lax.fori_loop(1, SPANS, push, 0)
        wait_for(far.at[r, pl.ds(0, SPANS - 1)], far_recv.at[r])
        table = far[r].reshape(SPANS * 48, 128)
        if r == 0:
            sums = combine(table, picks2[...], weights2[...])
            near[1, g] = place(first + sums + pltpu.roll(sums, 64, axis=1))
            push_near(1)
            halos[2].wait_recv()
            halos[3].wait_recv()
            prepare(faces_ref, low_ref, high_ref, spacing_ref, lhs_ref, fns_ref)
            for copy in results:
                copy.start()
        else:
            state = combine(table, picks[...], weights[...])
    skel_ref[...] = state
    for copy in results:
        copy.wait()
    wait_for(send.at[pl.ds(0, GROUPS - 1)], send_sem)
    for halo in halos:
        halo.wait_send()
    wait_for(near_rows.at[pl.ds(0, GROUPS - 1)], rows_send.at[0])
    wait_for(far_rows.at[pl.ds(0, SPANS - 1)], rows_send.at[1])
    for r in range(ROUNDS):
        wait_for(near.at[r, pl.ds(0, GROUPS - 1)], near_send.at[r])
        wait_for(far.at[r, pl.ds(0, SPANS - 1)], far_send.at[r])


def front(disp, weight, owner, row, force, coupling, stiff, edges, spacing):
    dma = pltpu.SemaphoreType.DMA
    local = [pltpu.VMEM(x.shape, x.dtype) for x in (disp, weight, owner, row, force, coupling, stiff, edges)]
    any_spec = pl.BlockSpec(memory_space=pl.ANY)
    lhs, fns = (CHUNKS, 12 * LAYERS, 128), (6, 3, LAYERS, 128)
    return pl.pallas_call(
        front_body,
        name="front",
        out_shape=(
            jax.ShapeDtypeStruct(lhs, BF16),
            jax.ShapeDtypeStruct(fns, F32),
            jax.ShapeDtypeStruct((8, 128), F32),
        ),
        in_specs=[any_spec] * 9,
        out_specs=(any_spec, any_spec, VMEM_SPEC),
        scratch_shapes=[
            *local, pltpu.SMEM(spacing.shape, F32),
            pltpu.VMEM((3, 256, 128), F32), pltpu.VMEM((3, 32, 128), F32), pltpu.VMEM((3, 32, 128), F32),
            pltpu.VMEM(lhs, BF16), pltpu.VMEM(fns, F32),
            pltpu.VMEM((512, NODES), BF16), pltpu.VMEM((256, NODES), BF16),
            pltpu.VMEM((GROUPS, 8, 256), F32), pltpu.VMEM((GROUPS, 8, 256), F32),
            pltpu.VMEM((6 * NP, 256), F32),
            pltpu.VMEM((16, 128), F32), pltpu.VMEM((16, 128), F32), pltpu.VMEM((16, 128), F32),
            pltpu.VMEM((2, 3, 32, 128), F32),
            pltpu.VMEM((ROUNDS, GROUPS, 4, 128), F32),
            pltpu.VMEM((ROUNDS, SPANS, 48, 128), F32),
            pltpu.VMEM((128, 896), BF16), pltpu.VMEM((128, 896), F32),
            pltpu.VMEM((GROUPS, 8, 128), F32), pltpu.VMEM((SPANS, 192, 128), F32),
            pltpu.VMEM((128, 2304), BF16), pltpu.VMEM((128, 2304), F32),
            dma((9,)), dma, dma((GROUPS,)),
            dma((ROUNDS,)), dma((ROUNDS,)), dma((ROUNDS,)), dma((ROUNDS,)), dma((4,)), dma((4,)),
            dma((2,)), dma((2,)), dma((2,)),
        ],
        compiler_params=pltpu.CompilerParams(
            collective_id=0, has_side_effects=True, vmem_limit_bytes=63 << 20
        ),
    )(disp, weight, owner, row, force, coupling, stiff, edges, spacing)


def place_bumps(skel_ref, lhs_ref):
    span = lax.axis_index("span")
    has_low = jnp.where(span > 0, 1.0, 0.0).astype(F32)
    has_high = jnp.where(span < SPANS - 1, 1.0, 0.0).astype(F32)
    lane, row = iota((LAYERS, 128), 1), iota((LAYERS, 128), 0)
    turn = row & 7
    for c in range(3):
        skel = jnp.broadcast_to(skel_ref[c : c + 1, :], (LAYERS, 128))

        def column(where):
            return jnp.sum(jnp.where(where, skel, 0.0), axis=1, keepdims=True)

        value = column(lane == row)
        nxt = column(lane == jnp.where(turn == 7, 64 + row - 7, row + 1))
        prv = column(lane == jnp.where(turn == 0, 64 + row + 7, row - 1))
        nxt = jnp.where(turn[:, 0:1] == 7, nxt * has_high, nxt)
        prv = jnp.where(turn[:, 0:1] == 0, prv * has_low, prv)
        diff = 0.5 * (nxt - prv)
        for n, (x, first) in enumerate(((value, 48), (value, 50), (value, 52), (diff, 48))):
            rows = slice((n * 3 + c) * LAYERS, (n * 3 + c + 1) * LAYERS)
            mine = (lane & 63 == first) | (lane & 63 == first + 1)
            high = x.astype(BF16).astype(F32)
            bump = jnp.where(mine, jnp.where(lane < 64, high, x - high), 0.0).astype(BF16)
            for chunk in range(CHUNKS):
                lhs_ref[chunk, rows, :] = lhs_ref[chunk, rows, :] + bump


def blend_body(
    lhs_hbm, fns_hbm, skel_hbm, table_hbm, disp_hbm, jac_hbm,
    lhs_ref, fns_ref, skel_ref, table_ref, picked, even, odd, disp_ref, jac_ref, load_sem, store_sem,
):
    loads = [
        pltpu.make_async_copy(src, dst, load_sem.at[n])
        for n, (src, dst) in enumerate(
            [(skel_hbm, skel_ref), (lhs_hbm, lhs_ref), (table_hbm, table_ref), (fns_hbm, fns_ref)]
        )
    ]
    for load in loads:
        load.start()
    loads[0].wait()
    loads[1].wait()
    place_bumps(skel_ref, lhs_ref)
    loads[2].wait()
    loads[3].wait()

    def cols_of(n):
        return pl.ds(pl.multiple_of(n * CHUNK, 128), CHUNK)

    def multiply(n, out):
        table = table_ref[:, cols_of(n)]
        out[...] = jnp.dot(lhs_ref[n], jnp.concatenate([table, table], axis=0), preferred_element_type=F32)

    def finish(n, found):
        place = iota((8, 128), 1)
        for phase in range(5):
            turns = []
            for turn in range(2):
                far = place + phase * 128
                j = n * CHUNK_J + turn * 8 + sum(jnp.where(far >= NP * k, 1, 0) for k in range(1, 8))
                t = j.astype(F32) * (1.0 / (NP - 1))
                t_j = jnp.where((j == 0) | (j == NP - 1), 0.5 / (NP - 1), 1.0 / (NP - 1))
                first = turn * 640 + phase * 128
                out_cols = pl.ds(pl.multiple_of(n * CHUNK + first, 128), 128)
                turns.append((t, t_j, slice(first, first + 128), out_cols))
            for q in range(8):
                lines = slice(q * 8, q * 8 + 8)
                fns = [[picked[phase, k, c, lines, :] for k in range(6)] for c in range(3)]
                for t, t_j, cols, out_cols in turns:
                    matrix = []
                    for c in range(3):
                        b, d, b_i, d_i, b_s, d_s = fns[c]
                        x, x_i, x_j, x_s = [
                            found[(k * 3 + c) * LAYERS + q * 8 : (k * 3 + c) * LAYERS + q * 8 + 8, cols]
                            for k in range(4)
                        ]
                        disp_ref[c, q, :, out_cols] = x + b + t * d
                        matrix.append([x_i + b_i + t * d_i, x_j + t_j * d, x_s + b_s + t * d_s])
                    one = matrix[1][1] * matrix[2][2] - matrix[1][2] * matrix[2][1]
                    two = matrix[1][0] * matrix[2][2] - matrix[1][2] * matrix[2][0]
                    three = matrix[1][0] * matrix[2][1] - matrix[1][1] * matrix[2][0]
                    jac_ref[q, :, out_cols] = matrix[0][0] * one - matrix[0][1] * two + matrix[0][2] * three

    def stores(n):
        cols = cols_of(n)
        return (
            pltpu.make_async_copy(disp_ref.at[:, :, :, cols], disp_hbm.at[:, :, :, cols], store_sem.at[0, n]),
            pltpu.make_async_copy(jac_ref.at[:, :, cols], jac_hbm.at[:, :, cols], store_sem.at[1, n]),
        )

    def start(n):
        for store in stores(n):
            store.start()

    multiply(0, even)
    lane = iota((8, 128), 1)
    for phase in range(5):
        at = lane + (phase * 128) % NP
        at = jnp.where(at >= NP, at - NP, at)
        at = jnp.where(at >= NP, at - NP, at)
        for n in range(6):
            for c in range(3):
                for q in range(8):
                    lines = slice(q * 8, q * 8 + 8)
                    picked[phase, n, c, lines, :] = jnp.take_along_axis(fns_ref[n, c, lines, :], at, axis=1)

    def step(k, carry):
        n = 2 * k
        multiply(n + 1, odd)
        finish(n, even)
        start(n)
        multiply(n + 2, even)
        finish(n + 1, odd)
        start(n + 1)
        return carry

    lax.fori_loop(0, CHUNKS // 2, step, 0)
    finish(CHUNKS - 1, even)
    start(CHUNKS - 1)

    def drain(n, carry):
        for store in stores(n):
            store.wait()
        return carry

    lax.fori_loop(0, CHUNKS, drain, 0)


def blend(lhs, fns, skel):
    any_spec = pl.BlockSpec(memory_space=pl.ANY)
    table = blend_table()
    return pl.pallas_call(
        blend_body,
        name="blend",
        out_shape=(
            jax.ShapeDtypeStruct((3, 8, 8, NP * NP), F32),
            jax.ShapeDtypeStruct((8, 8, NP * NP), F32),
        ),
        in_specs=[any_spec] * 4,
        out_specs=(any_spec, any_spec),
        scratch_shapes=[
            pltpu.VMEM(lhs.shape, BF16), pltpu.VMEM(fns.shape, F32), pltpu.VMEM(skel.shape, F32),
            pltpu.VMEM(table.shape, BF16), pltpu.VMEM((5, 6, 3, LAYERS, 128), F32),
            pltpu.VMEM((12 * LAYERS, CHUNK), F32), pltpu.VMEM((12 * LAYERS, CHUNK), F32),
            pltpu.VMEM((3, 8, 8, NP * NP), F32), pltpu.VMEM((8, 8, NP * NP), F32),
            pltpu.SemaphoreType.DMA((4,)), pltpu.SemaphoreType.DMA((2, CHUNKS)),
        ],
        compiler_params=pltpu.CompilerParams(vmem_limit_bytes=63 << 20),
    )(lhs, fns, skel, jnp.asarray(table))


def on_device(disp, weight, owner, row, force, coupling, stiff, edges, spacing):
    lhs, fns, skel = front(
        disp, weight.T, owner.T, row.T, force, coupling, stiff.reshape(1, -1), edges, spacing
    )
    return blend(lhs, fns, skel)


def solution(mesh):
    return jax.shard_map(
        on_device,
        mesh=mesh,
        in_specs=(
            P(None, ("group", "span")),
            P(("group", "span"), None),
            P(("group", "span"), None),
            P(("group", "span"), None),
            P(None, ("group", "span")),
            P(None, ("group", "span")),
            P(("group", "span")),
            P(None, ("group", "span")),
            P(None, "group"),
        ),
        out_specs=(P(None, "group", "span", None), P("group", "span", None)),
        check_vma=False,
    )
```

```python
import functools

import jax
import jax.numpy as jnp
import numpy as np
from jax import lax
from jax.experimental import pallas as pl
from jax.experimental.pallas import tpu as pltpu
from jax.sharding import PartitionSpec as P

F32, BF16, I32 = jnp.float32, jnp.bfloat16, jnp.int32
NP = 80
LAYERS = 64
GROUPS, SPANS = 32, 8
NODES = 2048
MESH = pl.DeviceIdType.MESH
NT = (((1,), (1,)), ((), ()))
VMEM_SPEC = pl.BlockSpec(memory_space=pltpu.VMEM)


def iota(shape, dim):
    return lax.broadcasted_iota(I32, shape, dim)


def split(value):
    high = value.astype(BF16)
    return high, (value - high.astype(F32)).astype(BF16)


CHUNK_J = 16
CHUNK = CHUNK_J * NP
CHUNKS = NP // CHUNK_J


def blend_table():
    f = np.arange(NP * NP)
    i, j = f % NP, f // NP
    n = NP - 1

    def bubble(i, j):
        s, t = i / n, j / n
        return 16.0 * s * (1 - s) * t * (1 - t)

    ip, im = np.minimum(i + 1, n), np.maximum(i - 1, 0)
    jp, jm = np.minimum(j + 1, n), np.maximum(j - 1, 0)
    hit = (j[None] % CHUNK_J == np.arange(CHUNK_J)[:, None]).astype(np.float64)
    rows = [hit, hit * i, hit * (ip - im)]
    for bump in (
        bubble(i, j), 0.5 * (bubble(ip, j) - bubble(im, j)), 0.5 * (bubble(i, jp) - bubble(i, jm))
    ):
        high = bump.astype(BF16).astype(np.float64)
        rows += [high[None], (bump - high)[None]]
    rows.append(np.zeros((10, NP * NP)))
    return np.concatenate(rows).astype(BF16)


def column_of(values):
    return jnp.concatenate([jnp.full((8, 128), value, F32) for value in values], axis=0)


def two_parts(x, lane):
    x = x + pltpu.roll(x, 64, axis=1)
    high = x.astype(BF16).astype(F32)
    return jnp.where(lane < 64, high, x - high).astype(BF16)


def prepare(faces_ref, low_ref, high_ref, spacing_ref, lhs_ref, fns_ref):
    span = lax.axis_index("span")
    has_low = jnp.where(span > 0, 1.0, 0.0).astype(F32)
    has_high = jnp.where(span < SPANS - 1, 1.0, 0.0).astype(F32)
    lane = iota((LAYERS, 128), 1)
    turn = iota((LAYERS, 128), 0) & 7
    frac = lane.astype(F32) * (1.0 / (NP - 1))

    def along_span(x, c, seg):
        rows = [slice(seg * 8 + q, seg * 8 + q + 1) for q in range(8)]
        before = jnp.concatenate([jnp.broadcast_to(low_ref[c, r, :], (8, 128)) for r in rows], axis=0)
        after = jnp.concatenate([jnp.broadcast_to(high_ref[c, r, :], (8, 128)) for r in rows], axis=0)
        nxt = jnp.where(turn == 7, after * has_high, pltpu.roll(x, LAYERS - 1, axis=0))
        prv = jnp.where(turn == 0, before * has_low, pltpu.roll(x, 1, axis=0))
        return 0.5 * (nxt - prv)

    def along_lane(x):
        nxt = jnp.where(lane == NP - 1, x, pltpu.roll(x, 127, axis=1))
        prv = jnp.where(lane == 0, x, pltpu.roll(x, 1, axis=1))
        return 0.5 * (nxt - prv)

    def inner(x):
        return x - (1.0 - frac) * x[:, 0:1] - frac * x[:, NP - 1 : NP]

    for c in range(3):
        now = [faces_ref[c, seg * LAYERS : (seg + 1) * LAYERS, :] for seg in range(4)]
        diff = [along_span(x, c, seg) for seg, x in enumerate(now)]
        values = []
        for bottom, top, left, right in (now, diff):
            base = inner(bottom)
            values.append((base, inner(top) - base, left, (right - left) * (1.0 / (NP - 1))))
        (b, d, left, m), (b_s, d_s, left_s, m_s) = values
        b_i, left_j = along_lane(b), along_lane(left)
        if c == 0:
            b_i = b_i + column_of([spacing_ref[c, q] for q in range(8)])
        elif c == 1:
            left_j = left_j + column_of([spacing_ref[c, q] for q in range(8)])
        else:
            b_s = b_s + column_of([spacing_ref[c, q] for q in range(8)])
        for n, fn in enumerate((b, d, b_i, along_lane(d), b_s, d_s)):
            fns_ref[n, c] = fn
        m_j = along_lane(m)
        for chunk in range(CHUNKS):

            def at(x, first):
                shift = (first - chunk * CHUNK_J) % 128
                return pltpu.roll(x, shift, axis=1) if shift else x

            fields = [
                jnp.where(lane < 16, at(x, 0), jnp.where(lane < 32, at(y, 16), 0.0))
                for x, y in ((left, m), (left_j, m_j), (left_s, m_s))
            ]
            fields.insert(1, jnp.where((lane >= 32) & (lane < 48), at(0.5 * m, 32), 0.0))
            for n, field in enumerate(fields):
                lhs_ref[chunk, (n * 3 + c) * LAYERS : (n * 3 + c + 1) * LAYERS, :] = two_parts(field, lane)


def wait_for(ref, sem):
    pltpu.make_async_copy(ref, ref, sem).wait()


def offset_peer(g, k):
    n, m = k // 4, k % 4
    dz = 4 + ((n + 1) // 2) * (1 - 2 * (n % 2))
    dx = 2 + ((m + 1) // 2) * (1 - 2 * (m % 2))
    return ((g // 8 + dx) % 4) * 8 + (g % 8 + dz) % 8


def pack(disp_ref, weight_ref, owner_ref, row_ref, out_ref, lhs, rhs):
    group_rows = iota((GROUPS, NODES), 0)
    present = jnp.zeros((GROUPS, NODES), F32)
    for t in range(4):
        present += jnp.where(owner_ref[t : t + 1, :] == group_rows, 1.0, 0.0)
    present = present.astype(BF16)
    before = jnp.where(iota((256, 256), 0) < iota((256, 256), 1), 1.0, 0.0).astype(BF16)
    every = jnp.ones((256, 256), BF16)
    base = jnp.zeros((GROUPS, 256), F32)
    ranks = []
    for k in range(NODES // 256):
        piece = present[:, k * 256 : (k + 1) * 256]
        ranks.append(jnp.dot(piece, before, preferred_element_type=F32) + base)
        base += jnp.dot(piece, every, preferred_element_type=F32)
    rank = jnp.concatenate(ranks, axis=1)
    word = iota((8, NODES), 0) & 3

    def one(t, total):
        line_t = pl.ds(t, 1)
        owner = owner_ref[line_t, :]
        slot = jnp.sum(jnp.where(owner == group_rows, rank, 0.0), axis=0, keepdims=True).astype(I32)
        half = slot >> 8
        column = slot & 255
        bucket = owner * 2 + half
        row = row_ref[line_t, :]
        layer = ((row >> 6) * 205) >> 10
        edge = row - layer * (4 * NP)
        seg = ((edge >> 4) * 205) >> 10
        along = (edge - seg * NP) << 8
        line = seg * LAYERS + layer
        weight = weight_ref[line_t, :]
        value = jnp.where(
            word == 0, disp_ref[0:1, :], jnp.where(word == 1, disp_ref[1:2, :], disp_ref[2:3, :])
        ) * weight
        high = jnp.where(word == 3, along.astype(F32), value).astype(BF16)
        low = jnp.where(word == 3, line.astype(F32), value - high.astype(F32)).astype(BF16)
        high = jnp.concatenate([high] * 32, axis=0)
        low = jnp.concatenate([low] * 32, axis=0)
        hit = (iota((256, NODES), 0) >> 2) == bucket
        zero = jnp.zeros((), BF16)
        lhs[0:256, :] = jnp.where(hit, high, zero)
        lhs[256:512, :] = jnp.where(hit, low, zero)
        rhs[...] = jnp.where(iota((256, NODES), 0) == column, 1.0, 0.0).astype(BF16)
        return total + lax.dot_general(lhs[...], rhs[...], NT, preferred_element_type=F32)

    total = lax.fori_loop(0, 4, one, jnp.zeros((512, 256), F32))
    out_ref[...] = (total[0:256] + total[256:512]).reshape(GROUPS, 8, 256)


def add_up(recv_ref, sources):
    lines = iota((256, 256), 0)
    places = iota((NP, 256), 0)
    zero = jnp.zeros((), BF16)
    lhs, rhs = [], []
    for source in sources:
        for h in range(2):
            code = recv_ref[source, 4 * h + 3 : 4 * h + 4, :].astype(I32)
            hit = places == (code >> 8)
            parts = []
            for c in range(3):
                for part in split(recv_ref[source, 4 * h + c : 4 * h + c + 1, :]):
                    parts.append(jnp.where(hit, jnp.broadcast_to(part, (NP, 256)), zero))
            lhs.append(jnp.concatenate(parts, axis=0))
            rhs.append(jnp.where(lines == (code & 255), 1.0, 0.0).astype(BF16))
    return lax.dot_general(
        jnp.concatenate(lhs, axis=1), jnp.concatenate(rhs, axis=1), NT, preferred_element_type=F32
    )


ROUNDS = 2
TOGETHER = 4


def front_body(
    disp_hbm, weight_hbm, owner_hbm, row_hbm, force_hbm, coupling_hbm, stiff_hbm, edges_hbm,
    spacing_hbm, lhs_hbm, fns_hbm, skel_ref,
    disp_ref, weight_ref, owner_ref, row_ref, force_ref, coupling_ref, stiff_ref, edges_ref,
    spacing_ref, faces_ref, low_ref, high_ref, lhs_ref, fns_ref, lhs, rhs, send, recv, total,
    static, low_in, high_in, face_out, near, far, picks, weights, near_rows, far_rows, picks2, weights2,
    load_sem, send_sem, recv_sem, near_send, near_recv, far_send, far_recv, halo_send, halo_recv,
    rows_send, rows_recv, result_sem,
):
    g, s = lax.axis_index("group"), lax.axis_index("span")
    up, down = (s + 1) % SPANS, (s + SPANS - 1) % SPANS
    loads = [
        pltpu.make_async_copy(src, dst, load_sem.at[n])
        for n, (src, dst) in enumerate(
            [
                (owner_hbm, owner_ref), (row_hbm, row_ref), (disp_hbm, disp_ref), (weight_hbm, weight_ref),
                (coupling_hbm, coupling_ref), (stiff_hbm, stiff_ref), (edges_hbm, edges_ref), (force_hbm, force_ref),
                (spacing_hbm, spacing_ref),
            ]
        )
    ]
    for load in loads:
        load.start()
    barrier = pltpu.get_barrier_semaphore()

    def greet_group(k, carry):
        pl.semaphore_signal(barrier, inc=1, device_id=(offset_peer(g, k), s), device_id_type=MESH)
        return carry

    def greet_span(k, carry):
        pl.semaphore_signal(barrier, inc=1, device_id=(g, (s + k) % SPANS), device_id_type=MESH)
        return carry

    lax.fori_loop(0, GROUPS - 1, greet_group, 0)
    lax.fori_loop(1, SPANS, greet_span, 0)
    for load in loads:
        load.wait()
    diagonal = stiff_ref[...] + jnp.sum(coupling_ref[...], axis=0, keepdims=True)
    share_rows, edge_rows = coupling_ref[...] / diagonal, edges_ref[...].astype(F32)
    blank = jnp.zeros((6, 64), F32)
    static[0:6, :] = jnp.concatenate([share_rows, blank], axis=1)
    static[8:14, :] = jnp.concatenate([edge_rows, blank], axis=1)
    near_rows[g] = jnp.concatenate(
        [jnp.concatenate([share_rows, edge_rows], axis=1), jnp.zeros((2, 128), F32)], axis=0
    )
    pl.semaphore_wait(barrier, GROUPS - 1 + SPANS - 1)

    def push_near_rows(k, carry):
        pltpu.make_async_remote_copy(
            near_rows.at[g], near_rows.at[g], rows_send.at[0], rows_recv.at[0],
            device_id=(offset_peer(g, k), s), device_id_type=MESH,
        ).start()
        return carry

    lax.fori_loop(0, GROUPS - 1, push_near_rows, 0)
    pack(disp_ref, weight_ref, owner_ref, row_ref, send, lhs, rhs)

    def push_send(k, carry):
        peer = offset_peer(g, k)
        pltpu.make_async_remote_copy(
            send.at[peer], recv.at[g], send_sem, recv_sem.at[g], device_id=(peer, s), device_id_type=MESH
        ).start()
        return carry

    lax.fori_loop(0, GROUPS - 1, push_send, 0)
    own = pltpu.make_async_copy(send.at[g], recv.at[g], recv_sem.at[g])
    own.start()
    halos = [
        pltpu.make_async_remote_copy(
            src, dst, halo_send.at[n], halo_recv.at[n], device_id=(g, to), device_id_type=MESH
        )
        for n, (src, dst, to) in enumerate(
            [
                (static, low_in, up), (static, high_in, down),
                (face_out.at[0], low_ref, up), (face_out.at[1], high_ref, down),
            ]
        )
    ]
    halos[0].start()
    halos[1].start()
    total[...] = jnp.zeros_like(total)
    halos[0].wait_recv()
    halos[1].wait_recv()
    lane = iota((8, 128), 1)
    own_half, turn = lane < 64, lane & 7

    def extended(own, below, above):
        beyond = jnp.where(turn == 7, below, jnp.where(turn == 0, above, 0.0))
        return jnp.where(own_half, own, pltpu.roll(beyond, 64, axis=1))

    share, edges = [
        extended(static[rows, :], low_in[rows, :], high_in[rows, :]) for rows in (slice(0, 8), slice(8, 16))
    ]
    edges = edges.astype(I32)
    sublane = iota((128, 128), 0)

    def locate(node):
        group, span, local = node >> 9, (node >> 6) & 7, node & 63
        return span * 16 + (group >> 1), (group & 1) * 64 + local

    here = iota((1, 128), 1)
    below = (g * SPANS + down) * 64 + here - 64
    above = (g * SPANS + up) * 64 + here - 64
    itself = jnp.where(here < 64, (g * SPANS + s) * 64 + here, jnp.where((here & 7) == 7, below, above))
    for d in range(7):
        line, column = locate(edges[d : d + 1, :] if d < 6 else itself)
        cols = slice(d * 128, (d + 1) * 128)
        picks[:, cols] = jnp.where(sublane == column, 1.0, 0.0).astype(BF16)
        weights[:, cols] = jnp.where(sublane == line, share[d : d + 1, :] if d < 6 else 1.0, 0.0)

    wait_for(near_rows.at[pl.ds(0, GROUPS - 1)], rows_recv.at[0])
    for h in range(16):
        even, odd = near_rows[2 * h], near_rows[2 * h + 1]
        pair = jnp.where(own_half, even, pltpu.roll(odd, 64, axis=1))
        ends = jnp.where(own_half, pltpu.roll(even, 64, axis=1), odd)
        for d in range(6):
            far_rows[s, d * 16 + h : d * 16 + h + 1, :] = pair[d : d + 1, :]
            far_rows[s, 96 + d * 16 + h : 96 + d * 16 + h + 1, :] = ends[d : d + 1, :]

    def push_far_rows(k, carry):
        pltpu.make_async_remote_copy(
            far_rows.at[s], far_rows.at[s], rows_send.at[1], rows_recv.at[1],
            device_id=(g, (s + k) % SPANS), device_id_type=MESH,
        ).start()
        return carry

    lax.fori_loop(1, SPANS, push_far_rows, 0)

    def collect(m, carry):
        sources = [offset_peer(g, m * TOGETHER + u) for u in range(TOGETHER)]
        for source in sources:
            wait_for(recv.at[source], recv_sem.at[source])
        total[...] += add_up(recv, sources)
        return carry

    lax.fori_loop(0, GROUPS // TOGETHER, collect, 0)
    row = iota((8, 128), 0)
    first = jnp.zeros((8, 128), F32)
    for c in range(3):
        sums = total[2 * c * NP : (2 * c + 1) * NP, :] + total[(2 * c + 1) * NP : (2 * c + 2) * NP, :]
        load = jnp.sum(sums, axis=0, keepdims=True)
        load = load[:, 0:128] + load[:, 128:256]
        load = load + pltpu.roll(load, 64, axis=1)
        value = (force_ref[c : c + 1, :] + 0.25 * load[:, 0:64]) / diagonal
        first = jnp.where(row == c, jnp.concatenate([value, value], axis=1), first)
        total[2 * c * NP : (2 * c + 1) * NP, :] = sums
    def place(state):
        state = jnp.where(own_half, state, 0.0)
        return jnp.where(g % 2 == 1, pltpu.roll(state, 64, axis=1), state)[0:4, :]

    def push_near(r):
        def push(k, carry):
            pltpu.make_async_remote_copy(
                near.at[r, g], near.at[r, g], near_send.at[r], near_recv.at[r],
                device_id=(offset_peer(g, k), s), device_id_type=MESH,
            ).start()
            return carry

        lax.fori_loop(0, GROUPS - 1, push, 0)

    near[0, g] = place(first)
    push_near(0)
    for c in range(3):
        full = jnp.concatenate([total[2 * c * NP : (2 * c + 1) * NP, :], jnp.zeros((128 - NP, 256), F32)], axis=0)
        faces_ref[c] = full.T
    for c in range(3):
        face_out[0, c] = faces_ref[c, pl.ds(7, 32, stride=8), :]
        face_out[1, c] = faces_ref[c, pl.ds(0, 32, stride=8), :]
    halos[2].start()
    halos[3].start()
    wait_for(far_rows.at[pl.ds(0, SPANS - 1)], rows_recv.at[1])
    links = [static[8 + d : 9 + d, :].astype(I32) for d in range(6)]
    joint = [jnp.where(here < 64, links[2 * t], pltpu.roll(links[2 * t + 1], 64, axis=1)) for t in range(3)]
    parts = [static[d : d + 1, :] for d in range(6)]
    shares = [jnp.where(here < 64, parts[2 * t], pltpu.roll(parts[2 * t + 1], 64, axis=1)) for t in range(3)]
    rows_table = jnp.concatenate(split(far_rows[...].reshape(SPANS * 192, 128)), axis=1)
    for t in range(3):
        line, column = locate(joint[t])
        pick = jnp.where(sublane == column, 1.0, 0.0).astype(BF16)
        found = jnp.dot(rows_table, jnp.concatenate([pick, pick], axis=0), preferred_element_type=F32)
        found = found.reshape(SPANS, 12, 16, 128)
        mask = jnp.where(sublane == line, 1.0, 0.0).reshape(SPANS, 16, 128)
        for d in range(6):
            share2 = jnp.sum((found[:, d] * mask).reshape(128, 128), axis=0, keepdims=True)
            link2 = jnp.sum((found[:, 6 + d] * mask).reshape(128, 128), axis=0, keepdims=True)
            line2, column2 = locate(link2.astype(I32))
            cols = slice((t * 6 + d) * 128, (t * 6 + d + 1) * 128)
            picks2[:, cols] = jnp.where(sublane == column2, 1.0, 0.0).astype(BF16)
            weights2[:, cols] = jnp.where(sublane == line2, share2 * shares[t], 0.0)

    def combine(table, pick, weight):
        table = jnp.concatenate(split(table), axis=1)
        out = jnp.zeros((8, 128), F32)
        found = jnp.dot(table, jnp.concatenate([pick, pick], axis=0), preferred_element_type=F32)
        width = pick.shape[1]
        found = found.reshape(SPANS, 3, 16, width)
        weighted = weight.reshape(SPANS, 16, width)
        for c in range(3):
            sums = jnp.sum((found[:, c] * weighted).reshape(SPANS * 16, width), axis=0, keepdims=True)
            parts = [sums[:, d * 128 : (d + 1) * 128] for d in range(width // 128)]
            out = jnp.where(row == c, functools.reduce(jnp.add, parts), out)
        return out

    results = [
        pltpu.make_async_copy(lhs_ref, lhs_hbm, result_sem.at[0]),
        pltpu.make_async_copy(fns_ref, fns_hbm, result_sem.at[1]),
    ]
    for r in range(ROUNDS):
        wait_for(near.at[r, pl.ds(0, GROUPS - 1)], near_recv.at[r])
        for h in range(16):
            pair = near[r, 2 * h] + near[r, 2 * h + 1]
            for c in range(3):
                far[r, s, c * 16 + h : c * 16 + h + 1, :] = pair[c : c + 1, :]

        def push(k, carry):
            peer = (s + k) % SPANS
            pltpu.make_async_remote_copy(
                far.at[r, s], far.at[r, s], far_send.at[r], far_recv.at[r],
                device_id=(g, peer), device_id_type=MESH,
            ).start()
            return carry

        lax.fori_loop(1, SPANS, push, 0)
        wait_for(far.at[r, pl.ds(0, SPANS - 1)], far_recv.at[r])
        table = far[r].reshape(SPANS * 48, 128)
        if r == 0:
            sums = combine(table, picks2[...], weights2[...])
            near[1, g] = place(first + sums + pltpu.roll(sums, 64, axis=1))
            push_near(1)
            halos[2].wait_recv()
            halos[3].wait_recv()
            prepare(faces_ref, low_ref, high_ref, spacing_ref, lhs_ref, fns_ref)
            for copy in results:
                copy.start()
        else:
            state = combine(table, picks[...], weights[...])
    skel_ref[...] = state
    for copy in results:
        copy.wait()
    wait_for(send.at[pl.ds(0, GROUPS - 1)], send_sem)
    for halo in halos:
        halo.wait_send()
    wait_for(near_rows.at[pl.ds(0, GROUPS - 1)], rows_send.at[0])
    wait_for(far_rows.at[pl.ds(0, SPANS - 1)], rows_send.at[1])
    for r in range(ROUNDS):
        wait_for(near.at[r, pl.ds(0, GROUPS - 1)], near_send.at[r])
        wait_for(far.at[r, pl.ds(0, SPANS - 1)], far_send.at[r])


def front(disp, weight, owner, row, force, coupling, stiff, edges, spacing):
    dma = pltpu.SemaphoreType.DMA
    local = [pltpu.VMEM(x.shape, x.dtype) for x in (disp, weight, owner, row, force, coupling, stiff, edges)]
    any_spec = pl.BlockSpec(memory_space=pl.ANY)
    lhs, fns = (CHUNKS, 12 * LAYERS, 128), (6, 3, LAYERS, 128)
    return pl.pallas_call(
        front_body,
        name="front",
        out_shape=(
            jax.ShapeDtypeStruct(lhs, BF16),
            jax.ShapeDtypeStruct(fns, F32),
            jax.ShapeDtypeStruct((8, 128), F32),
        ),
        in_specs=[any_spec] * 9,
        out_specs=(any_spec, any_spec, VMEM_SPEC),
        scratch_shapes=[
            *local, pltpu.SMEM(spacing.shape, F32),
            pltpu.VMEM((3, 256, 128), F32), pltpu.VMEM((3, 32, 128), F32), pltpu.VMEM((3, 32, 128), F32),
            pltpu.VMEM(lhs, BF16), pltpu.VMEM(fns, F32),
            pltpu.VMEM((512, NODES), BF16), pltpu.VMEM((256, NODES), BF16),
            pltpu.VMEM((GROUPS, 8, 256), F32), pltpu.VMEM((GROUPS, 8, 256), F32),
            pltpu.VMEM((6 * NP, 256), F32),
            pltpu.VMEM((16, 128), F32), pltpu.VMEM((16, 128), F32), pltpu.VMEM((16, 128), F32),
            pltpu.VMEM((2, 3, 32, 128), F32),
            pltpu.VMEM((ROUNDS, GROUPS, 4, 128), F32),
            pltpu.VMEM((ROUNDS, SPANS, 48, 128), F32),
            pltpu.VMEM((128, 896), BF16), pltpu.VMEM((128, 896), F32),
            pltpu.VMEM((GROUPS, 8, 128), F32), pltpu.VMEM((SPANS, 192, 128), F32),
            pltpu.VMEM((128, 2304), BF16), pltpu.VMEM((128, 2304), F32),
            dma((9,)), dma, dma((GROUPS,)),
            dma((ROUNDS,)), dma((ROUNDS,)), dma((ROUNDS,)), dma((ROUNDS,)), dma((4,)), dma((4,)),
            dma((2,)), dma((2,)), dma((2,)),
        ],
        compiler_params=pltpu.CompilerParams(
            collective_id=0, has_side_effects=True, vmem_limit_bytes=63 << 20
        ),
    )(disp, weight, owner, row, force, coupling, stiff, edges, spacing)


def place_bumps(skel_ref, lhs_ref):
    span = lax.axis_index("span")
    has_low = jnp.where(span > 0, 1.0, 0.0).astype(F32)
    has_high = jnp.where(span < SPANS - 1, 1.0, 0.0).astype(F32)
    lane, row = iota((LAYERS, 128), 1), iota((LAYERS, 128), 0)
    turn = row & 7
    for c in range(3):
        skel = jnp.broadcast_to(skel_ref[c : c + 1, :], (LAYERS, 128))

        def column(where):
            return jnp.sum(jnp.where(where, skel, 0.0), axis=1, keepdims=True)

        value = column(lane == row)
        nxt = column(lane == jnp.where(turn == 7, 64 + row - 7, row + 1))
        prv = column(lane == jnp.where(turn == 0, 64 + row + 7, row - 1))
        nxt = jnp.where(turn[:, 0:1] == 7, nxt * has_high, nxt)
        prv = jnp.where(turn[:, 0:1] == 0, prv * has_low, prv)
        diff = 0.5 * (nxt - prv)
        for n, (x, first) in enumerate(((value, 48), (value, 50), (value, 52), (diff, 48))):
            rows = slice((n * 3 + c) * LAYERS, (n * 3 + c + 1) * LAYERS)
            mine = (lane & 63 == first) | (lane & 63 == first + 1)
            high = x.astype(BF16).astype(F32)
            bump = jnp.where(mine, jnp.where(lane < 64, high, x - high), 0.0).astype(BF16)
            for chunk in range(CHUNKS):
                lhs_ref[chunk, rows, :] = lhs_ref[chunk, rows, :] + bump


def blend_body(
    lhs_hbm, fns_hbm, skel_hbm, table_hbm, disp_hbm, jac_hbm,
    lhs_ref, fns_ref, skel_ref, table_ref, picked, even, odd, disp_ref, jac_ref, load_sem, store_sem,
):
    loads = [
        pltpu.make_async_copy(src, dst, load_sem.at[n])
        for n, (src, dst) in enumerate(
            [(skel_hbm, skel_ref), (lhs_hbm, lhs_ref), (table_hbm, table_ref), (fns_hbm, fns_ref)]
        )
    ]
    for load in loads:
        load.start()
    loads[0].wait()
    loads[1].wait()
    place_bumps(skel_ref, lhs_ref)
    loads[2].wait()
    loads[3].wait()

    def cols_of(n):
        return pl.ds(pl.multiple_of(n * CHUNK, 128), CHUNK)

    def multiply(n, out):
        table = table_ref[:, cols_of(n)]
        out[...] = jnp.dot(lhs_ref[n], jnp.concatenate([table, table], axis=0), preferred_element_type=F32)

    def finish(n, found):
        place = iota((8, 128), 1)
        for phase in range(5):
            turns = []
            for turn in range(2):
                far = place + phase * 128
                j = n * CHUNK_J + turn * 8 + sum(jnp.where(far >= NP * k, 1, 0) for k in range(1, 8))
                t = j.astype(F32) * (1.0 / (NP - 1))
                t_j = jnp.where((j == 0) | (j == NP - 1), 0.5 / (NP - 1), 1.0 / (NP - 1))
                first = turn * 640 + phase * 128
                out_cols = pl.ds(pl.multiple_of(n * CHUNK + first, 128), 128)
                turns.append((t, t_j, slice(first, first + 128), out_cols))
            for q in range(8):
                lines = slice(q * 8, q * 8 + 8)
                fns = [[picked[phase, k, c, lines, :] for k in range(6)] for c in range(3)]
                for t, t_j, cols, out_cols in turns:
                    matrix = []
                    for c in range(3):
                        b, d, b_i, d_i, b_s, d_s = fns[c]
                        x, x_i, x_j, x_s = [
                            found[(k * 3 + c) * LAYERS + q * 8 : (k * 3 + c) * LAYERS + q * 8 + 8, cols]
                            for k in range(4)
                        ]
                        disp_ref[c, q, :, out_cols] = x + b + t * d
                        matrix.append([x_i + b_i + t * d_i, x_j + t_j * d, x_s + b_s + t * d_s])
                    one = matrix[1][1] * matrix[2][2] - matrix[1][2] * matrix[2][1]
                    two = matrix[1][0] * matrix[2][2] - matrix[1][2] * matrix[2][0]
                    three = matrix[1][0] * matrix[2][1] - matrix[1][1] * matrix[2][0]
                    jac_ref[q, :, out_cols] = matrix[0][0] * one - matrix[0][1] * two + matrix[0][2] * three

    def stores(n):
        cols = cols_of(n)
        return (
            pltpu.make_async_copy(disp_ref.at[:, :, :, cols], disp_hbm.at[:, :, :, cols], store_sem.at[0, n]),
            pltpu.make_async_copy(jac_ref.at[:, :, cols], jac_hbm.at[:, :, cols], store_sem.at[1, n]),
        )

    def start(n):
        for store in stores(n):
            store.start()

    multiply(0, even)
    lane = iota((8, 128), 1)
    for phase in range(5):
        at = lane + (phase * 128) % NP
        at = jnp.where(at >= NP, at - NP, at)
        at = jnp.where(at >= NP, at - NP, at)
        for n in range(6):
            for c in range(3):
                for q in range(8):
                    lines = slice(q * 8, q * 8 + 8)
                    picked[phase, n, c, lines, :] = jnp.take_along_axis(fns_ref[n, c, lines, :], at, axis=1)

    def step(k, carry):
        n = 2 * k
        multiply(n + 1, odd)
        finish(n, even)
        start(n)
        multiply(n + 2, even)
        finish(n + 1, odd)
        start(n + 1)
        return carry

    lax.fori_loop(0, CHUNKS // 2, step, 0)
    finish(CHUNKS - 1, even)
    start(CHUNKS - 1)

    def drain(n, carry):
        for store in stores(n):
            store.wait()
        return carry

    lax.fori_loop(0, CHUNKS, drain, 0)


def blend(lhs, fns, skel):
    any_spec = pl.BlockSpec(memory_space=pl.ANY)
    table = blend_table()
    return pl.pallas_call(
        blend_body,
        name="blend",
        out_shape=(
            jax.ShapeDtypeStruct((3, 8, 8, NP * NP), F32),
            jax.ShapeDtypeStruct((8, 8, NP * NP), F32),
        ),
        in_specs=[any_spec] * 4,
        out_specs=(any_spec, any_spec),
        scratch_shapes=[
            pltpu.VMEM(lhs.shape, BF16), pltpu.VMEM(fns.shape, F32), pltpu.VMEM(skel.shape, F32),
            pltpu.VMEM(table.shape, BF16), pltpu.VMEM((5, 6, 3, LAYERS, 128), F32),
            pltpu.VMEM((12 * LAYERS, CHUNK), F32), pltpu.VMEM((12 * LAYERS, CHUNK), F32),
            pltpu.VMEM((3, 8, 8, NP * NP), F32), pltpu.VMEM((8, 8, NP * NP), F32),
            pltpu.SemaphoreType.DMA((4,)), pltpu.SemaphoreType.DMA((2, CHUNKS)),
        ],
        compiler_params=pltpu.CompilerParams(vmem_limit_bytes=63 << 20),
    )(lhs, fns, skel, jnp.asarray(table))


def on_device(disp, weight, owner, row, force, coupling, stiff, edges, spacing):
    lhs, fns, skel = front(
        disp, weight.T, owner.T, row.T, force, coupling, stiff.reshape(1, -1), edges, spacing
    )
    return blend(lhs, fns, skel)


def solution(mesh):
    return jax.shard_map(
        on_device,
        mesh=mesh,
        in_specs=(
            P(None, ("group", "span")),
            P(("group", "span"), None),
            P(("group", "span"), None),
            P(("group", "span"), None),
            P(None, ("group", "span")),
            P(None, ("group", "span")),
            P(("group", "span")),
            P(None, ("group", "span")),
            P(None, "group"),
        ),
        out_specs=(P(None, "group", "span", None), P("group", "span", None)),
        check_vma=False,
    )
```
